256 devices in a mesh: rows: 8 (over y_hi, x), cols: 32 (over y_lo, z, core).
Axes of the slice: x: 4, y: 4 (y_hi: 2, y_lo: 2; y = y_hi * 2 + y_lo), z: 8, core: 2. Of those that a mesh axis runs over, the one named last changes fastest.
Arguments:
- coarse_one: bfloat16 [64, 2048, 128], P('rows', 'cols'), may hold values from -100 to 100
- coarse_two: bfloat16 [64, 2048, 128], P('rows', 'cols'), may hold values from -100 to 100
- fine_one: bfloat16 [128, 4096, 128], P('rows', 'cols'), may hold values from -100 to 100
- fine_two: bfloat16 [128, 4096, 128], P('rows', 'cols'), may hold values from -100 to 100
- selection: int32 [8, 32, 12, 32], P('rows', 'cols'), may hold values from 0 to 1, as said below
- counts: int32 [8, 32], P('rows', 'cols'), may hold values from 1 to 12, as said below
Outputs:
- coarse_flow: float32 [2, 64, 2048], P(None, 'rows', 'cols')
- refined_flow: float32 [2, 128, 4096], P(None, 'rows', 'cols')
The draws below stay inside these ranges and needn't reach their ends.
Inputs may be any that keep to these rules, and one draw needn't show every extreme that they name: `selection`: each slot row is one-hot; slot 0 of tile (r, c) names its own panel c; the first counts[r, c] slots name distinct panels; later slots name arbitrary panels. `counts`: some tile has 12 valid slots.
All inputs are finite; a program needn't handle non-finite values.
Results may differ from the reference program's by a relative error of at most 0.0003.
Values may be sent and summed in bfloat16 or wider, within the bound.
A program may use at most 128 MiB of HBM per device.

```python
import jax
import jax.numpy as jnp
from jax import lax

C = 128
R8 = 8
P8 = 64
RADIUS = 4
SLOTS = 12
H8 = 64
W8 = 2048
H4 = 128
W4 = 4096
N_ROWS = 8
N_COLS = 32


def slot_counts(key):
    tile_count = N_ROWS * N_COLS
    first_pick = jax.random.randint(jax.random.fold_in(key, 22), (tile_count,), 1, SLOTS + 1)
    second_pick = jax.random.randint(jax.random.fold_in(key, 23), (tile_count,), 1, SLOTS + 1)
    fewest = jnp.minimum(first_pick, second_pick)
    busiest = jax.random.randint(jax.random.fold_in(key, 24), (), 0, tile_count)
    return jnp.where(jnp.arange(tile_count, dtype=jnp.int32) == busiest, SLOTS, fewest).astype(jnp.int32)


def candidate_panels(key):
    tile_count = N_ROWS * N_COLS
    tile_keys = jax.random.split(jax.random.fold_in(key, 21), tile_count)
    offsets = jax.vmap(lambda single: jax.random.permutation(single, N_COLS - 1) + 1)(tile_keys)
    offsets = jnp.concatenate([jnp.zeros((tile_count, 1), jnp.int32), offsets[:, :SLOTS - 1].astype(jnp.int32)], axis=1)
    own_panel = jnp.arange(tile_count, dtype=jnp.int32) % N_COLS
    panels = (own_panel[:, None] + offsets) % N_COLS
    filler = jax.random.randint(jax.random.fold_in(key, 25), (tile_count, SLOTS), 0, N_COLS)
    valid_slots = slot_counts(key)
    alive = jnp.arange(SLOTS, dtype=jnp.int32)[None, :] < valid_slots[:, None]
    panels = jnp.where(alive, panels, filler).astype(jnp.int32)
    return (panels, valid_slots)


def feature_pair(key, height, width, channels, target_row, target_col, low, high):
    base_two = jnp.clip(jax.random.normal(jax.random.fold_in(key, 1), (height, width, channels), jnp.float32), -5.0, 5.0)
    base_one = jnp.clip(jax.random.normal(jax.random.fold_in(key, 2), (height, width, channels), jnp.float32), -5.0, 5.0)
    second = base_two
    strength = jax.random.uniform(jax.random.fold_in(key, 6), (height, width, 1), jnp.float32, low, high)
    first = base_one + strength * second[target_row, target_col]
    return (first, second)


def coarse_targets(key):
    panels, valid_slots = candidate_panels(key)
    row_ids = jnp.arange(H8, dtype=jnp.int32)[:, None] + jnp.zeros((H8, W8), jnp.int32)
    col_ids = jnp.arange(W8, dtype=jnp.int32)[None, :] + jnp.zeros((H8, W8), jnp.int32)
    tile = row_ids // R8 * N_COLS + col_ids // P8
    slot = jax.random.randint(jax.random.fold_in(key, 31), (H8, W8), 0, valid_slots[tile])
    panel = panels[tile, slot]
    target_row = row_ids // R8 * R8 + jax.random.randint(jax.random.fold_in(key, 32), (H8, W8), 0, R8)
    target_col = panel * P8 + jax.random.randint(jax.random.fold_in(key, 33), (H8, W8), 0, P8)
    return (target_row, target_col)


def fine_targets(key):
    row_ids = jnp.arange(H4, dtype=jnp.int32)[:, None] + jnp.zeros((H4, W4), jnp.int32)
    col_ids = jnp.arange(W4, dtype=jnp.int32)[None, :] + jnp.zeros((H4, W4), jnp.int32)
    row_step = jax.random.randint(jax.random.fold_in(key, 41), (H4, W4), -RADIUS, RADIUS + 1)
    col_step = jax.random.randint(jax.random.fold_in(key, 42), (H4, W4), -RADIUS, RADIUS + 1)
    target_row = jnp.clip(row_ids + row_step, 0, H4 - 1)
    target_col = jnp.clip(col_ids + col_step, 0, W4 - 1)
    return (target_row, target_col)


def coarse_pair(key):
    target_row, target_col = coarse_targets(key)
    return feature_pair(jax.random.fold_in(key, 11), H8, W8, C, target_row, target_col, 0.6, 1.2)


def fine_pair(key):
    target_row, target_col = fine_targets(key)
    return feature_pair(jax.random.fold_in(key, 12), H4, W4, C, target_row, target_col, 0.3, 0.8)


def draw_coarse_one(key, part):
    return coarse_pair(key)[0].astype(jnp.bfloat16)


def draw_coarse_two(key, part):
    return coarse_pair(key)[1].astype(jnp.bfloat16)


def draw_fine_one(key, part):
    return fine_pair(key)[0].astype(jnp.bfloat16)


def draw_fine_two(key, part):
    return fine_pair(key)[1].astype(jnp.bfloat16)


def draw_counts(key, part):
    return slot_counts(key).reshape(N_ROWS, N_COLS)


def draw_selection(key, part):
    panels, valid_slots = candidate_panels(key)
    onehot = (panels[:, :, None] == jnp.arange(N_COLS, dtype=jnp.int32)[None, None, :]).astype(jnp.int32)
    return onehot.reshape(N_ROWS, N_COLS, SLOTS, N_COLS)


def setup_inputs(seed: int = 0) -> dict:
    arg_keys = jax.random.split(jax.random.key(seed), 7)
    coarse_one = draw_coarse_one(jax.random.fold_in(arg_keys[6], 71), 0)
    coarse_two = draw_coarse_two(jax.random.fold_in(arg_keys[6], 71), 0)
    fine_one = draw_fine_one(jax.random.fold_in(arg_keys[6], 71), 0)
    fine_two = draw_fine_two(jax.random.fold_in(arg_keys[6], 71), 0)
    selection = draw_selection(jax.random.fold_in(arg_keys[6], 71), 0)
    counts = draw_counts(jax.random.fold_in(arg_keys[6], 71), 0)
    return dict(coarse_one=coarse_one, coarse_two=coarse_two, fine_one=fine_one, fine_two=fine_two, selection=selection, counts=counts)


def reference(coarse_one, coarse_two, fine_one, fine_two, selection, counts):
    inv_root = 1.0 / (C ** 0.5)
    unit_len = 4.0 * P8
    tile_cells = R8 * P8
    tile_count = N_ROWS * N_COLS
    tiles_one = coarse_one.reshape(N_ROWS, R8, N_COLS, P8, C).transpose(0, 2, 1, 3, 4).reshape(tile_count, tile_cells, C)
    tiles_two = coarse_two.reshape(N_ROWS, R8, N_COLS, P8, C).transpose(0, 2, 1, 3, 4).reshape(N_ROWS, N_COLS, tile_cells, C)
    cell_ids = jnp.arange(tile_cells, dtype=jnp.int32)
    local_row = (cell_ids // P8).astype(jnp.float32)
    local_col = (cell_ids % P8).astype(jnp.float32)
    panel_ids = jnp.arange(N_COLS, dtype=jnp.int32)
    slot_ids = jnp.arange(SLOTS, dtype=jnp.int32)
    tile_ids = jnp.arange(tile_count, dtype=jnp.int32)

    def one_tile(packed):
        tile_id, queries, chosen, count_now = packed
        band = tile_id // N_COLS
        column = tile_id % N_COLS
        panels = jnp.sum(chosen * panel_ids[None, :], axis=1).astype(jnp.int32)
        key_rows = tiles_two[band][panels]
        scores = jnp.einsum("qc,skc->qsk", queries.astype(jnp.float32), key_rows.astype(jnp.float32)) * inv_root
        alive = slot_ids < count_now
        scores = jnp.where(alive[None, :, None], scores, -jnp.inf)
        highest = jnp.max(scores, axis=(1, 2), keepdims=True)
        weights = jnp.exp(scores - highest)
        total_weight = jnp.sum(weights, axis=(1, 2))
        key_col = panels.astype(jnp.float32)[:, None] * P8 + local_col[None, :]
        sum_col = jnp.sum(weights * key_col[None, :, :], axis=(1, 2))
        sum_row = jnp.sum(weights * local_row[None, None, :], axis=(1, 2))
        query_col = column.astype(jnp.float32) * P8 + local_col
        flow_x = (sum_col / total_weight - query_col) / unit_len
        flow_y = (sum_row / total_weight - local_row) / unit_len
        return jnp.stack([flow_x, flow_y])

    flows = lax.map(one_tile, (tile_ids, tiles_one, selection.reshape(tile_count, SLOTS, N_COLS), counts.reshape(tile_count)))
    coarse_flow = flows.reshape(N_ROWS, N_COLS, 2, R8, P8).transpose(2, 0, 3, 1, 4).reshape(2, H8, W8)

    upsampled = jnp.repeat(jnp.repeat(coarse_flow, 2, axis=1), 2, axis=2)
    span = 2 * RADIUS + 1
    padded_two = jnp.pad(fine_two, ((RADIUS, RADIUS), (RADIUS, RADIUS), (0, 0)))
    padded_flow = jnp.pad(upsampled, ((0, 0), (RADIUS, RADIUS), (RADIUS, RADIUS)))
    first_field = fine_one.astype(jnp.float32)

    def offset_step(index, carry):
        running_max, total_weight, accum = carry
        row_shift = (index // span).astype(jnp.int32)
        col_shift = (index % span).astype(jnp.int32)
        shifted = lax.dynamic_slice(padded_two, (row_shift, col_shift, jnp.int32(0)), (H4, W4, C))
        score = jnp.sum(first_field * shifted.astype(jnp.float32), axis=-1) * inv_root
        flow_here = lax.dynamic_slice(padded_flow, (jnp.int32(0), row_shift, col_shift), (2, H4, W4))
        new_max = jnp.maximum(running_max, score)
        decay = jnp.exp(running_max - new_max)
        weight = jnp.exp(score - new_max)
        return new_max, total_weight * decay + weight, accum * decay[None] + weight[None] * flow_here

    start = (jnp.full((H4, W4), -jnp.inf, jnp.float32), jnp.zeros((H4, W4), jnp.float32), jnp.zeros((2, H4, W4), jnp.float32))
    running_max, total_weight, accum = lax.fori_loop(0, span * span, offset_step, start)
    refined_flow = accum / total_weight[None]
    return coarse_flow, refined_flow
```

```python
import functools

import jax
import jax.numpy as jnp
import numpy as np
from jax import lax
from jax.experimental import pallas as pl
from jax.experimental.pallas import tpu as pltpu
from jax.sharding import PartitionSpec as P

MESH = pl.DeviceIdType.MESH
F32 = jnp.float32
BF16 = jnp.bfloat16
NROWS, NCOLS = 8, 32
NZ = 8
CH = 128
BH, BW = 8, 64
FH, FW = 16, 128
RAD = 4
PAD = 8
SCALE = float(np.log2(np.e) / np.sqrt(128.0))
LOW = -1.0e30
NEIGHBOURS = [(dy, dx) for dy in (-1, 0, 1) for dx in (-1, 0, 1) if (dy, dx) != (0, 0)]
NT = (((1,), (1,)), ((), ()))


def spans(d, size, halo):
    if d == 0:
        return 0, size, halo
    if d == 1:
        return size - halo, halo, 0
    return 0, halo, size + halo


def kernel(
    c1, c2, f1, f2, sel, cnt,
    coarse_out, fine_out,
    kb, qb, f1v, ext, wbuf, maskb, pscr, lv, biasb, acc, st_tx, st_rx, fl, ft,
    ring_send, ring_recv, q_send, q_recv, lv_send, lv_recv, halo_send, halo_recv,
    st_send, st_recv, fl_send, fl_recv, loc,
):
    r = lax.axis_index("rows")
    c = lax.axis_index("cols")
    ylo = c // 16
    z = (c // 2) % NZ
    core = c % 2

    def at_z(zz):
        return (r, ylo * 16 + zz * 2 + core)

    ring_to = (at_z((z + 1) % NZ), at_z((z + NZ - 1) % NZ))

    def partner(j):
        return (r, ((ylo + j // 2) % 2) * 16 + z * 2 + (core + j % 2) % 2)

    def neighbour(dy, dx):
        return ((r + dy + NROWS) % NROWS, (c + dx + NCOLS) % NCOLS)

    everyone = list(ring_to) + [partner(j) for j in (1, 2, 3)] + [neighbour(*n) for n in NEIGHBOURS]

    own_k = pltpu.make_async_copy(c2, kb.at[0:2], loc.at[0])
    own_q = pltpu.make_async_copy(c1, qb.at[0], loc.at[1])
    own_f1 = pltpu.make_async_copy(f1, f1v, loc.at[2])
    own_f2 = pltpu.make_async_copy(f2, ext.at[RAD : RAD + FH, PAD : PAD + FW], loc.at[3])
    for copy in (own_k, own_q, own_f1, own_f2):
        copy.start()

    slot = lax.broadcasted_iota(jnp.int32, (12, NCOLS), 0)
    chosen = jnp.where(slot < cnt[...], sel[0, 0], 0)
    live = jnp.sum(chosen.astype(F32), axis=0, keepdims=True)
    lv[0] = jnp.broadcast_to(jnp.concatenate([live, jnp.zeros((1, 128 - NCOLS), F32)], axis=1), (8, 128))

    barrier = pltpu.get_barrier_semaphore()
    for device in everyone:
        pl.semaphore_signal(barrier, inc=1, device_id=device, device_id_type=MESH)
    pl.semaphore_wait(barrier, len(everyone))

    def ring(way, d, h, source):
        return pltpu.make_async_remote_copy(
            src_ref=source, dst_ref=kb.at[2 + (d * 2 + h) * 2 + way],
            send_sem=ring_send.at[way, d, h], recv_sem=ring_recv.at[way, d, h],
            device_id=ring_to[way], device_id_type=MESH,
        )

    for h in range(2):
        for way in range(2):
            ring(way, 0, h, c2.at[h]).start()

    def share(j, source, target, send, recv):
        return pltpu.make_async_remote_copy(
            src_ref=source, dst_ref=target, send_sem=send.at[j - 1], recv_sem=recv.at[j - 1],
            device_id=partner(j), device_id_type=MESH,
        )

    lives = [share(j, lv.at[0], lv.at[j], lv_send, lv_recv) for j in (1, 2, 3)]
    asks = [share(j, c1, qb.at[j], q_send, q_recv) for j in (1, 2, 3)]
    for copy in asks + lives:
        copy.start()

    halos = []
    for i, (dy, dx) in enumerate(NEIGHBOURS):
        ys, yn, yt = spans(dy, FH, RAD)
        xs, xn, xt = spans(dx, FW, PAD)
        halos.append(
            pltpu.make_async_remote_copy(
                src_ref=f2.at[ys : ys + yn, xs : xs + xn], dst_ref=ext.at[yt : yt + yn, xt : xt + xn],
                send_sem=halo_send.at[i], recv_sem=halo_recv.at[i],
                device_id=neighbour(dy, dx), device_id_type=MESH,
            )
        )
    for copy in halos:
        copy.start()

    key = lax.broadcasted_iota(jnp.int32, (512, 128), 0)
    query = lax.broadcasted_iota(jnp.int32, (512, 128), 1)
    off_y = key // 32 - RAD - query // 16
    off_x = key % 32 - PAD - query % 16
    inside = (jnp.abs(off_y) <= RAD) & (jnp.abs(off_x) <= RAD)
    maskb[...] = jnp.where(inside, 0.0, LOW)

    for j in range(4):
        acc[j, 0] = jnp.full((8, 512), LOW, F32)
        for s in (1, 2, 3):
            acc[j, s] = jnp.zeros((8, 512), F32)

    def set_bias(j):
        lane = lax.broadcasted_iota(jnp.int32, (NCOLS, 128), 1)
        panel = lax.broadcasted_iota(jnp.int32, (NCOLS, 128), 0)
        column = jnp.sum(jnp.where(lane == panel, lv[j][0:1, :], 0.0), axis=1, keepdims=True)
        biasb[j] = jnp.broadcast_to((1.0 - column) * (2.0 * LOW), (NCOLS, 256))

    set_bias(0)
    own_k.wait()
    own_q.wait()
    own_f1.wait()
    own_f2.wait()
    for copy in asks + lives:
        copy.wait_recv()
    for j in (1, 2, 3):
        set_bias(j)

    def match(at, panel, h):
        keys = kb[at].reshape(4 * BW, CH)
        base = (panel * BW).astype(F32)
        first_row = (h * 4).astype(F32)

        def tile(i, _):
            j, half = i // 2, i % 2
            lanes = pl.ds(pl.multiple_of(half * 256, 256), 256)
            queries = qb[j, half].reshape(256, CH)
            score = lax.dot_general(keys, queries, NT, preferred_element_type=F32)
            score = score.reshape(4, 8, 8, 256)
            top = jnp.max(score, axis=(0, 1))
            weight = jnp.exp2((score - top) * SCALE)
            by_row = [functools.reduce(jnp.add, [weight[y, v] for v in range(8)]) for y in range(4)]
            by_col = [functools.reduce(jnp.add, [weight[y, v] for y in range(4)]) for v in range(8)]
            total = (by_row[0] + by_row[1]) + (by_row[2] + by_row[3])
            in_row = by_row[1] + 2.0 * by_row[2] + 3.0 * by_row[3] + first_row * total
            in_col = functools.reduce(jnp.add, [(8.0 * v) * by_col[v] for v in range(1, 8)]) + base * total
            seen = top + biasb[j, pl.ds(panel, 1), :]
            before = acc[j, 0, :, lanes]
            now = jnp.maximum(before, seen)
            keep = jnp.exp2((before - now) * SCALE)
            take = jnp.exp2((seen - now) * SCALE)
            acc[j, 0, :, lanes] = now
            acc[j, 1, :, lanes] = keep * acc[j, 1, :, lanes] + take * total
            acc[j, 2, :, lanes] = keep * acc[j, 2, :, lanes] + take * in_col
            acc[j, 3, :, lanes] = keep * acc[j, 3, :, lanes] + take * in_row
            return 0

        lax.fori_loop(0, 8, tile, 0)

    def window(b):
        by, bx = b // 8, b % 8
        rows = pl.ds(by * 8, 16)
        keys = ext[rows, pl.ds(pl.multiple_of(bx * 16, 16), 32), :].reshape(512, CH)
        queries = f1v[pl.ds(by * 8, 8), pl.ds(pl.multiple_of(bx * 16, 16), 16), :].reshape(128, CH)
        score = lax.dot_general(keys, queries, NT, preferred_element_type=F32) + maskb[...]
        top = jnp.max(score, axis=0, keepdims=True)
        weight = jnp.exp2((score - top) * SCALE)
        total = jnp.sum(weight, axis=0, keepdims=True)
        pairs = weight.reshape(8, 2, 32, 128)
        pairs = (pairs[:, 0] + pairs[:, 1]) * (1.0 / total)
        pscr[...] = pairs.reshape(256, 128)
        wbuf[b] = pscr[pl.ds(0, 128, stride=2), :] + pscr[pl.ds(1, 128, stride=2), :]

    def step(t, _):
        d, h = (t + 1) // 2 - 1, (t + 1) % 2

        @pl.when(t >= 1)
        def _():
            for way in range(2):

                @pl.when((d < 3) | (h == way))
                def _():
                    ring(way, d, h, kb.at[0]).wait_recv()

                    @pl.when((d < 2) | ((d == 2) & (h == way)))
                    def _():
                        ring(way, d + 1, h, kb.at[2 + (d * 2 + h) * 2 + way]).start()

        def chunk(way, _):
            own = t == 0

            @pl.when(own | (d < 3) | (h == way))
            def _():
                zs = jnp.where(own, z, (z + NZ + (2 * way - 1) * (d + 1)) % NZ)
                match(2 * t + way, ylo * 16 + zs * 2 + core, jnp.where(own, way, h))

            return 0

        lax.fori_loop(0, 2, chunk, 0)

        @pl.when(t == 1)
        def _():
            for copy in halos:
                copy.wait_recv()

            @pl.when(r == 0)
            def _():
                ext[0:RAD] = jnp.zeros((RAD, FW + 2 * PAD, CH), BF16)

            @pl.when(r == NROWS - 1)
            def _():
                ext[RAD + FH :] = jnp.zeros((RAD, FW + 2 * PAD, CH), BF16)

            @pl.when(c == 0)
            def _():
                ext[:, 0:PAD] = jnp.zeros((FH + 2 * RAD, PAD, CH), BF16)

            @pl.when(c == NCOLS - 1)
            def _():
                ext[:, PAD + FW :] = jnp.zeros((FH + 2 * RAD, PAD, CH), BF16)

        @pl.when(t >= 1)
        def _():
            window(2 * t - 2)
            window(2 * t - 1)

        return 0

    lax.fori_loop(0, 9, step, 0)

    sub = lax.broadcasted_iota(jnp.int32, (8, 512), 0).astype(F32)

    def moments(j):
        top8, total, in_col, in_row = acc[j, 0], acc[j, 1], acc[j, 2], acc[j, 3]
        in_col = in_col + sub * total
        top = jnp.max(top8, axis=0, keepdims=True)
        part = jnp.exp2((top8 - top) * SCALE)
        sums = [jnp.sum(part * v, axis=0, keepdims=True) for v in (total, in_col, in_row)]
        return jnp.concatenate([top] + sums + [jnp.zeros((4, 512), F32)], axis=0)

    backs = [share(j, st_tx.at[j - 1], st_rx.at[j - 1], st_send, st_recv) for j in (1, 2, 3)]
    for j in (3, 2, 1):
        st_tx[j - 1] = moments(j)
        backs[j - 1].start()
    parts = [moments(0)]
    for j in (1, 2, 3):
        backs[j - 1].wait_recv()
        parts.append(st_rx[j - 1])
    top = functools.reduce(jnp.maximum, [p[0:1] for p in parts])
    scales = [jnp.exp2((p[0:1] - top) * SCALE) for p in parts]
    total, in_col, in_row = (
        functools.reduce(jnp.add, [s * p[i : i + 1] for s, p in zip(scales, parts)]) for i in (1, 2, 3)
    )
    cell = lax.broadcasted_iota(jnp.int32, (1, 512), 1)
    query_col = (c * BW + cell % BW).astype(F32)
    query_row = (cell // BW).astype(F32)
    flow_x = (in_col / total - query_col) * (1.0 / 256.0)
    flow_y = (in_row / total - query_row) * (1.0 / 256.0)
    flow = jnp.concatenate([f[:, 128 * i : 128 * i + 128] for f in (flow_x, flow_y) for i in range(4)], axis=0)
    fl[1, 1] = flow
    coarse_out[...] = flow
    edges = []
    for i, (dy, dx) in enumerate(NEIGHBOURS):
        edges.append(
            pltpu.make_async_remote_copy(
                src_ref=fl.at[1, 1], dst_ref=fl.at[1 - dy, 1 - dx],
                send_sem=fl_send.at[i], recv_sem=fl_recv.at[i],
                device_id=neighbour(dy, dx), device_id_type=MESH,
            )
        )
    for copy in edges:
        copy.start()
    for copy in edges:
        copy.wait_recv()

    tiles = {}
    for ty in range(3):
        for tx in range(3):
            tile = fl[ty, tx]
            outside = []
            if ty == 0:
                outside.append(r == 0)
            if ty == 2:
                outside.append(r == NROWS - 1)
            if tx == 0:
                outside.append(c == 0)
            if tx == 2:
                outside.append(c == NCOLS - 1)
            for gone in outside:
                tile = tile * jnp.where(gone, 0.0, 1.0)
            tiles[ty, tx] = tile

    i72 = lax.broadcasted_iota(jnp.int32, (72, 128), 0)
    lane = lax.broadcasted_iota(jnp.int32, (72, 128), 1)
    goal = jnp.where(i72 < 4, 60 + i72, jnp.where(i72 < 68, i72 - 4, i72 - 68))
    for e in range(12):
        ty = 0 if e < 2 else (1 if e < 10 else 2)
        row = (e - 2) % 8
        hit = lane == goal + (row % 2) * 64
        for k in range(2):
            at = k * 4 + row // 2
            left, mid, right = (tiles[ty, tx][at : at + 1, :] for tx in range(3))
            pick = jnp.where(i72 < 4, left, jnp.where(i72 < 68, mid, right))
            ft[k, e] = jnp.broadcast_to(
                jnp.sum(jnp.where(hit, pick, 0.0), axis=1, keepdims=True), (72, 128)
            )

    for b in range(16):
        by, bx = b // 8, b % 8
        weight = wbuf[b].reshape(8, 16, 128)
        for k in range(2):
            value = ft[k, by * 4 : by * 4 + 8, bx * 8 : bx * 8 + 16, :]
            fine_out[k, b : b + 1, :] = jnp.sum((weight * value).reshape(128, 128), axis=0, keepdims=True)

    for h in range(2):
        for way in range(2):
            for d in range(4):
                if d < 3 or h == way:
                    ring(way, d, h, kb.at[0]).wait_send()
    for copy in asks + lives + halos + backs + edges:
        copy.wait_send()


def local(coarse_one, coarse_two, fine_one, fine_two, selection, counts):
    vm = pltpu.VMEM
    dma = pltpu.SemaphoreType.DMA
    any_spec = pl.BlockSpec(memory_space=pl.ANY)
    vm_spec = pl.BlockSpec(memory_space=pltpu.VMEM)
    coarse, fine = pl.pallas_call(
        kernel,
        out_shape=(jax.ShapeDtypeStruct((8, 128), F32), jax.ShapeDtypeStruct((2, 16, 128), F32)),
        in_specs=[any_spec] * 4 + [vm_spec] * 2,
        out_specs=(vm_spec, vm_spec),
        scratch_shapes=[
            vm((18, 4, BW, CH), BF16),
            vm((4, 2, 4, BW, CH), BF16),
            vm((FH, FW, CH), BF16),
            vm((FH + 2 * RAD, FW + 2 * PAD, CH), BF16),
            vm((16, 128, 128), F32),
            vm((512, 128), F32),
            vm((256, 128), F32),
            vm((4, 8, 128), F32),
            vm((4, NCOLS, 256), F32),
            vm((4, 4, 8, 512), F32),
            vm((3, 8, 512), F32),
            vm((3, 8, 512), F32),
            vm((3, 3, 8, 128), F32),
            vm((2, 12, 72, 128), F32),
            dma((2, 4, 2)), dma((2, 4, 2)),
            dma((3,)), dma((3,)), dma((3,)), dma((3,)),
            dma((8,)), dma((8,)),
            dma((3,)), dma((3,)),
            dma((8,)), dma((8,)),
            dma((4,)),
        ],
        compiler_params=pltpu.CompilerParams(collective_id=0, has_side_effects=True, vmem_limit_bytes=48 << 20),
        name="flow",
    )(
        coarse_one.reshape(2, 4, BW, CH), coarse_two.reshape(2, 4, BW, CH), fine_one, fine_two, selection, counts
    )
    coarse = coarse.reshape(2, BH, BW)
    fine = fine.reshape(2, 2, 8, 8, 16).transpose(0, 1, 3, 2, 4).reshape(2, FH, FW)
    return coarse, fine


def solution(mesh):
    return jax.shard_map(
        local,
        mesh=mesh,
        in_specs=(
            P("rows", "cols", None),
            P("rows", "cols", None),
            P("rows", "cols", None),
            P("rows", "cols", None),
            P("rows", "cols", None, None),
            P("rows", "cols"),
        ),
        out_specs=(P(None, "rows", "cols"), P(None, "rows", "cols")),
        check_vma=False,
    )
```

```python
import functools

import jax
import jax.numpy as jnp
import numpy as np
from jax import lax
from jax.experimental import pallas as pl
from jax.experimental.pallas import tpu as pltpu
from jax.sharding import PartitionSpec as P

MESH = pl.DeviceIdType.MESH
F32 = jnp.float32
BF16 = jnp.bfloat16
NROWS, NCOLS = 8, 32
NZ = 8
CH = 128
BH, BW = 8, 64
FH, FW = 16, 128
RAD = 4
PAD = 8
SCALE = float(np.log2(np.e) / np.sqrt(128.0))
LOW = -1.0e30
NEIGHBOURS = [(dy, dx) for dy in (-1, 0, 1) for dx in (-1, 0, 1) if (dy, dx) != (0, 0)]
NT = (((1,), (1,)), ((), ()))


def spans(d, size, halo):
    if d == 0:
        return 0, size, halo
    if d == 1:
        return size - halo, halo, 0
    return 0, halo, size + halo


def kernel(
    c1, c2, f1, f2, sel, cnt,
    coarse_out, fine_out,
    kb, qb, q2, f1v, ext, wbuf, maskb, pscr, selv, cntv, lv, biasb, acc, st_tx, st_rx, fl, ft,
    ring_send, ring_recv, q_send, q_recv, lv_send, lv_recv, halo_send, halo_recv,
    st_send, st_recv, fl_send, fl_recv, loc,
):
    r = lax.axis_index("rows")
    c = lax.axis_index("cols")
    ylo = c // 16
    z = (c // 2) % NZ
    core = c % 2

    def at_z(zz):
        return (r, ylo * 16 + zz * 2 + core)

    ring_to = (at_z((z + 1) % NZ), at_z((z + NZ - 1) % NZ))

    def partner(j):
        return (r, ((ylo + j // 2) % 2) * 16 + z * 2 + (core + j % 2) % 2)

    def neighbour(dy, dx):
        return ((r + dy + NROWS) % NROWS, (c + dx + NCOLS) % NCOLS)

    def exists(dy, dx):
        there = True
        for d, at, last in ((dy, r, NROWS - 1), (dx, c, NCOLS - 1)):
            if d == -1:
                there = there & (at > 0)
            if d == 1:
                there = there & (at < last)
        return there

    def each(copies, what):
        for copy, (dy, dx) in zip(copies, NEIGHBOURS):
            there = exists(-dy, -dx) if what == "wait_recv" else exists(dy, dx)

            @pl.when(there)
            def _(copy=copy):
                getattr(copy, what)()

    everyone = list(ring_to) + [partner(j) for j in (1, 2, 3)] + [neighbour(*n) for n in NEIGHBOURS]

    own_sel = pltpu.make_async_copy(sel, selv, loc.at[4])
    own_cnt = pltpu.make_async_copy(cnt, cntv, loc.at[5])
    own_k = pltpu.make_async_copy(c2, kb.at[0], loc.at[0])
    own_q = pltpu.make_async_copy(c1, qb.at[0], loc.at[1])
    own_f1 = pltpu.make_async_copy(f1, f1v, loc.at[2])
    own_f2 = pltpu.make_async_copy(f2, ext.at[RAD : RAD + FH, PAD : PAD + FW], loc.at[3])
    for copy in (own_sel, own_cnt, own_k, own_q, own_f1, own_f2):
        copy.start()

    fl[...] = jnp.zeros((3, 3, 8, 128), F32)

    @pl.when(r == 0)
    def _():
        ext[0:RAD] = jnp.zeros((RAD, FW + 2 * PAD, CH), BF16)

    @pl.when(r == NROWS - 1)
    def _():
        ext[RAD + FH :] = jnp.zeros((RAD, FW + 2 * PAD, CH), BF16)

    @pl.when(c == 0)
    def _():
        ext[:, 0:PAD] = jnp.zeros((FH + 2 * RAD, PAD, CH), BF16)

    @pl.when(c == NCOLS - 1)
    def _():
        ext[:, PAD + FW :] = jnp.zeros((FH + 2 * RAD, PAD, CH), BF16)

    barrier = pltpu.get_barrier_semaphore()
    for device in everyone:
        pl.semaphore_signal(barrier, inc=1, device_id=device, device_id_type=MESH)
    pl.semaphore_wait(barrier, len(everyone))

    def ring(way, d, h, source):
        return pltpu.make_async_remote_copy(
            src_ref=source, dst_ref=kb.at[jnp.minimum(1 + 2 * d + way, 7), h],
            send_sem=ring_send.at[way, d, h], recv_sem=ring_recv.at[way, d, h],
            device_id=ring_to[way], device_id_type=MESH,
        )

    for h in range(2):
        for way in range(2):
            ring(way, 0, h, c2.at[h]).start()

    def share(j, source, target, send, recv):
        return pltpu.make_async_remote_copy(
            src_ref=source, dst_ref=target, send_sem=send.at[j - 1], recv_sem=recv.at[j - 1],
            device_id=partner(j), device_id_type=MESH,
        )

    lives = [share(j, lv.at[0], lv.at[j], lv_send, lv_recv) for j in (1, 2, 3)]
    asks = [share(j, c1, qb.at[j], q_send, q_recv) for j in (1, 2, 3)]
    for copy in asks:
        copy.start()

    own_sel.wait()
    own_cnt.wait()
    slot = lax.broadcasted_iota(jnp.int32, (12, 1, NCOLS), 0)
    chosen = jnp.where(slot < cntv[...].reshape(1, 1, 1), selv[...], 0)
    live = jnp.sum(chosen.astype(F32), axis=0)
    lv[0] = jnp.broadcast_to(jnp.concatenate([live, jnp.zeros((1, 128 - NCOLS), F32)], axis=1), (8, 128))

    for copy in lives:
        copy.start()

    halos = []
    for i, (dy, dx) in enumerate(NEIGHBOURS):
        ys, yn, yt = spans(dy, FH, RAD)
        xs, xn, xt = spans(dx, FW, PAD)
        halos.append(
            pltpu.make_async_remote_copy(
                src_ref=f2.at[ys : ys + yn, xs : xs + xn], dst_ref=ext.at[yt : yt + yn, xt : xt + xn],
                send_sem=halo_send.at[i], recv_sem=halo_recv.at[i],
                device_id=neighbour(dy, dx), device_id_type=MESH,
            )
        )
    each(halos, "start")

    key = lax.broadcasted_iota(jnp.int32, (512, 128), 0)
    query = lax.broadcasted_iota(jnp.int32, (512, 128), 1)
    off_y = key // 32 - RAD - query // 16
    off_x = key % 32 - PAD - query % 16
    inside = (jnp.abs(off_y) <= RAD) & (jnp.abs(off_x) <= RAD)
    maskb[...] = jnp.where(inside, 0.0, LOW)

    for j in range(4):
        acc[j, 0] = jnp.full((8, 512), LOW, F32)
        for s in (1, 2, 3):
            acc[j, s] = jnp.zeros((8, 512), F32)

    def set_bias(j):
        lane = lax.broadcasted_iota(jnp.int32, (NCOLS, 128), 1)
        panel = lax.broadcasted_iota(jnp.int32, (NCOLS, 128), 0)
        column = jnp.sum(jnp.where(lane == panel, lv[j][0:1, :], 0.0), axis=1, keepdims=True)
        biasb[j] = jnp.broadcast_to((1.0 - column) * (2.0 * LOW), (NCOLS, 256))

    def split(j):
        q = qb[j].reshape(BH * BW, CH).astype(F32) * SCALE
        high = q.astype(BF16)
        q2[j] = jnp.concatenate([high, (q - high.astype(F32)).astype(BF16)], axis=1)

    set_bias(0)
    own_q.wait()
    split(0)
    own_k.wait()
    own_f1.wait()
    own_f2.wait()
    for j in (1, 2, 3):
        lives[j - 1].wait_recv()
        set_bias(j)
        asks[j - 1].wait_recv()
        split(j)

    def match(at, panel):
        keys = kb[at].reshape(BH * BW, CH)
        keys = jnp.concatenate([keys, keys], axis=1)
        base = (panel * BW).astype(F32)
        for j in range(4):
            for lanes in (pl.ds(0, 256), pl.ds(256, 256)):
                score = lax.dot_general(keys, q2[j, lanes, :], NT, preferred_element_type=F32)
                score = score.reshape(64, 8, 256)
                top = jnp.max(score, axis=0)
                level = [jnp.exp2(score[i] - top) for i in range(64)]
                odd = []
                while len(level) > 1:
                    odd.append(functools.reduce(jnp.add, level[1::2]))
                    level = [a + b for a, b in zip(level[0::2], level[1::2])]
                total = level[0]
                in_col = 8.0 * (odd[0] + 2.0 * odd[1] + 4.0 * odd[2]) + base * total
                in_row = odd[3] + 2.0 * odd[4] + 4.0 * odd[5]
                seen = top + biasb[j, pl.ds(panel, 1), :]
                before = acc[j, 0, :, lanes]
                now = jnp.maximum(before, seen)
                keep = jnp.exp2(before - now)
                take = jnp.exp2(seen - now)
                acc[j, 0, :, lanes] = now
                acc[j, 1, :, lanes] = keep * acc[j, 1, :, lanes] + take * total
                acc[j, 2, :, lanes] = keep * acc[j, 2, :, lanes] + take * in_col
                acc[j, 3, :, lanes] = keep * acc[j, 3, :, lanes] + take * in_row

    def window(b):
        by, bx = b // 8, b % 8
        rows = pl.ds(by * 8, 16)
        keys = ext[rows, pl.ds(pl.multiple_of(bx * 16, 16), 32), :].reshape(512, CH)
        queries = f1v[pl.ds(by * 8, 8), pl.ds(pl.multiple_of(bx * 16, 16), 16), :].reshape(128, CH)
        score = lax.dot_general(keys, queries, NT, preferred_element_type=F32) + maskb[...]
        top = jnp.max(score, axis=0, keepdims=True)
        weight = jnp.exp2((score - top) * SCALE)
        total = jnp.sum(weight, axis=0, keepdims=True)
        pairs = weight.reshape(8, 2, 32, 128)
        pairs = (pairs[:, 0] + pairs[:, 1]) * (1.0 / total)
        pscr[...] = pairs.reshape(256, 128)
        wbuf[b] = pscr[pl.ds(0, 128, stride=2), :] + pscr[pl.ds(1, 128, stride=2), :]

    def ready_windows():
        each(halos, "wait_recv")

    def two_windows(i, _):
        window(2 * i)
        window(2 * i + 1)
        return 0

    def step(p, _):
        @pl.when(p < 6)
        def _():
            d, h = p // 2, p % 2
            for way in range(2):
                ring(way, d, h, kb.at[0, 0]).wait_recv()

                @pl.when((d < 2) | (h == way))
                def _(way=way):
                    ring(way, d + 1, h, kb.at[1 + 2 * d + way, h]).start()

        @pl.when(p == 7)
        def _():
            for way in range(2):
                ring(way, 3, way, kb.at[0, 0]).wait_recv()

        depth = (p + 1) // 2
        sign = jnp.where(p == 7, -1, 1 - 2 * (p % 2))
        zs = (z + NZ + sign * depth) % NZ
        match(p, ylo * 16 + zs * 2 + core)
        return 0

    lax.fori_loop(0, 8, step, 0)

    sub = lax.broadcasted_iota(jnp.int32, (8, 512), 0).astype(F32)

    def moments(j):
        top8, total, in_col, in_row = acc[j, 0], acc[j, 1], acc[j, 2], acc[j, 3]
        in_col = in_col + sub * total
        top = jnp.max(top8, axis=0, keepdims=True)
        part = jnp.exp2(top8 - top)
        sums = [jnp.sum(part * v, axis=0, keepdims=True) for v in (total, in_col, in_row)]
        return jnp.concatenate([top] + sums + [jnp.zeros((4, 512), F32)], axis=0)

    backs = [share(j, st_tx.at[j - 1], st_rx.at[j - 1], st_send, st_recv) for j in (1, 2, 3)]
    for j in (3, 2, 1):
        st_tx[j - 1] = moments(j)
        backs[j - 1].start()
    parts = [moments(0)]
    ready_windows()
    lax.fori_loop(0, 4, two_windows, 0)
    for j in (1, 2, 3):
        backs[j - 1].wait_recv()
        parts.append(st_rx[j - 1])
    top = functools.reduce(jnp.maximum, [p[0:1] for p in parts])
    scales = [jnp.exp2(p[0:1] - top) for p in parts]
    total, in_col, in_row = (
        functools.reduce(jnp.add, [s * p[i : i + 1] for s, p in zip(scales, parts)]) for i in (1, 2, 3)
    )
    cell = lax.broadcasted_iota(jnp.int32, (1, 512), 1)
    query_col = (c * BW + cell % BW).astype(F32)
    query_row = (cell // BW).astype(F32)
    flow_x = (in_col / total - query_col) * (1.0 / 256.0)
    flow_y = (in_row / total - query_row) * (1.0 / 256.0)
    flow = jnp.concatenate([f[:, 128 * i : 128 * i + 128] for f in (flow_x, flow_y) for i in range(4)], axis=0)
    fl[1, 1] = flow
    coarse_out[...] = flow
    edges = []
    for i, (dy, dx) in enumerate(NEIGHBOURS):
        edges.append(
            pltpu.make_async_remote_copy(
                src_ref=fl.at[1, 1], dst_ref=fl.at[1 - dy, 1 - dx],
                send_sem=fl_send.at[i], recv_sem=fl_recv.at[i],
                device_id=neighbour(dy, dx), device_id_type=MESH,
            )
        )
    each(edges, "start")
    lax.fori_loop(4, 8, two_windows, 0)
    each(edges, "wait_recv")

    tiles = {}
    for ty in range(3):
        for tx in range(3):
            tiles[ty, tx] = fl[ty, tx]

    i72 = lax.broadcasted_iota(jnp.int32, (72, 128), 0)
    lane = lax.broadcasted_iota(jnp.int32, (72, 128), 1)
    goal = jnp.where(i72 < 4, 60 + i72, jnp.where(i72 < 68, i72 - 4, i72 - 68))
    for e in range(12):
        ty = 0 if e < 2 else (1 if e < 10 else 2)
        row = (e - 2) % 8
        hit = lane == goal + (row % 2) * 64
        for k in range(2):
            at = k * 4 + row // 2
            left, mid, right = (tiles[ty, tx][at : at + 1, :] for tx in range(3))
            pick = jnp.where(i72 < 4, left, jnp.where(i72 < 68, mid, right))
            ft[k, e] = jnp.broadcast_to(
                jnp.sum(jnp.where(hit, pick, 0.0), axis=1, keepdims=True), (72, 128)
            )

    for b in range(16):
        by, bx = b // 8, b % 8
        weight = wbuf[b].reshape(8, 16, 128)
        for k in range(2):
            value = ft[k, by * 4 : by * 4 + 8, bx * 8 : bx * 8 + 16, :]
            fine_out[k, b : b + 1, :] = jnp.sum((weight * value).reshape(128, 128), axis=0, keepdims=True)

    for h in range(2):
        for way in range(2):
            for d in range(4):
                if d < 3 or h == way:
                    ring(way, d, h, kb.at[0, 0]).wait_send()
    for copy in asks + lives + backs:
        copy.wait_send()
    each(halos, "wait_send")
    each(edges, "wait_send")


def local(coarse_one, coarse_two, fine_one, fine_two, selection, counts):
    vm = pltpu.VMEM
    dma = pltpu.SemaphoreType.DMA
    any_spec = pl.BlockSpec(memory_space=pl.ANY)
    vm_spec = pl.BlockSpec(memory_space=pltpu.VMEM)
    coarse, fine = pl.pallas_call(
        kernel,
        out_shape=(jax.ShapeDtypeStruct((8, 128), F32), jax.ShapeDtypeStruct((2, 16, 128), F32)),
        in_specs=[any_spec] * 5 + [pl.BlockSpec(memory_space=pltpu.HBM)],
        out_specs=(vm_spec, vm_spec),
        scratch_shapes=[
            vm((8, 2, 4, BW, CH), BF16),
            vm((4, 2, 4, BW, CH), BF16),
            vm((4, BH * BW, 2 * CH), BF16),
            vm((FH, FW, CH), BF16),
            vm((FH + 2 * RAD, FW + 2 * PAD, CH), BF16),
            vm((16, 128, 128), F32),
            vm((512, 128), F32),
            vm((256, 128), F32),
            vm((12, 1, NCOLS), jnp.int32),
            vm((1, 1), jnp.int32),
            vm((4, 8, 128), F32),
            vm((4, NCOLS, 256), F32),
            vm((4, 4, 8, 512), F32),
            vm((3, 8, 512), F32),
            vm((3, 8, 512), F32),
            vm((3, 3, 8, 128), F32),
            vm((2, 12, 72, 128), F32),
            dma((2, 4, 2)), dma((2, 4, 2)),
            dma((3,)), dma((3,)), dma((3,)), dma((3,)),
            dma((8,)), dma((8,)),
            dma((3,)), dma((3,)),
            dma((8,)), dma((8,)),
            dma((6,)),
        ],
        compiler_params=pltpu.CompilerParams(collective_id=0, has_side_effects=True, vmem_limit_bytes=63 << 20),
        name="flow",
    )(
        coarse_one.reshape(2, 4, BW, CH), coarse_two.reshape(2, 4, BW, CH), fine_one, fine_two,
        selection.reshape(12, 1, NCOLS), counts
    )
    coarse = coarse.reshape(2, BH, BW)
    fine = fine.reshape(2, 2, 8, 8, 16).transpose(0, 1, 3, 2, 4).reshape(2, FH, FW)
    return coarse, fine


def solution(mesh):
    return jax.shard_map(
        local,
        mesh=mesh,
        in_specs=(
            P("rows", "cols", None),
            P("rows", "cols", None),
            P("rows", "cols", None),
            P("rows", "cols", None),
            P("rows", "cols", None, None),
            P("rows", "cols"),
        ),
        out_specs=(P(None, "rows", "cols"), P(None, "rows", "cols")),
        check_vma=False,
    )
```

```python
import functools

import jax
import jax.numpy as jnp
import numpy as np
from jax import lax
from jax.experimental import pallas as pl
from jax.experimental.pallas import tpu as pltpu
from jax.sharding import PartitionSpec as P

MESH = pl.DeviceIdType.MESH
F32 = jnp.float32
BF16 = jnp.bfloat16
NROWS, NCOLS = 8, 32
NZ = 8
NH = 2
CH = 128
BH, BW = 8, 64
FH, FW = 16, 128
RAD = 4
PAD = 8
SCALE = float(np.log2(np.e) / np.sqrt(128.0))
LOW = -1.0e30
NEIGHBOURS = [(dy, dx) for dy in (-1, 0, 1) for dx in (-1, 0, 1) if (dy, dx) != (0, 0)]
NT = (((1,), (1,)), ((), ()))


def spans(d, size, halo):
    if d == 0:
        return 0, size, halo
    if d == 1:
        return size - halo, halo, 0
    return 0, halo, size + halo


def kernel(
    c1, c2, f1, f2, sel, cnt,
    coarse_out, fine_out,
    kb, qb, q2, f1v, ext, wbuf, maskb, pscr, selv, cntv, lv, biasb, acc, st_tx, st_rx, fl, ft, part_sum,
    ring_send, ring_recv, q_send, q_recv, lv_send, lv_recv, halo_send, halo_recv,
    st_send, st_recv, fl_send, fl_recv, loc,
):
    r = lax.axis_index("rows")
    c = lax.axis_index("cols")
    ylo = c // 16
    z = (c // 2) % NZ
    core = c % 2

    def at_z(zz):
        return (r, ylo * 16 + zz * 2 + core)

    ring_to = (at_z((z + 1) % NZ), at_z((z + NZ - 1) % NZ))

    def partner(j):
        return (r, ((ylo + j // 2) % 2) * 16 + z * 2 + (core + j % 2) % 2)

    def neighbour(dy, dx):
        return ((r + dy + NROWS) % NROWS, (c + dx + NCOLS) % NCOLS)

    def exists(dy, dx):
        there = True
        for d, at, last in ((dy, r, NROWS - 1), (dx, c, NCOLS - 1)):
            if d == -1:
                there = there & (at > 0)
            if d == 1:
                there = there & (at < last)
        return there

    def each(copies, what):
        for copy, (dy, dx) in zip(copies, NEIGHBOURS):
            there = exists(-dy, -dx) if what == "wait_recv" else exists(dy, dx)

            @pl.when(there)
            def _(copy=copy):
                getattr(copy, what)()

    everyone = list(ring_to) + [partner(j) for j in (1, 2, 3)] + [neighbour(*n) for n in NEIGHBOURS]

    own_sel = pltpu.make_async_copy(sel, selv, loc.at[4])
    own_cnt = pltpu.make_async_copy(cnt, cntv, loc.at[5])
    own_k = pltpu.make_async_copy(c2, kb.at[0], loc.at[0])
    own_q = pltpu.make_async_copy(c1, qb.at[0], loc.at[1])
    own_f1 = pltpu.make_async_copy(f1, f1v, loc.at[2])
    own_f2 = pltpu.make_async_copy(f2, ext.at[RAD : RAD + FH, PAD : PAD + FW], loc.at[3])
    for copy in (own_sel, own_cnt, own_k, own_q, own_f1, own_f2):
        copy.start()

    fl[...] = jnp.zeros((3, 3, 8, 128), F32)

    @pl.when(r == 0)
    def _():
        ext[0:RAD] = jnp.zeros((RAD, FW + 2 * PAD, CH), BF16)

    @pl.when(r == NROWS - 1)
    def _():
        ext[RAD + FH :] = jnp.zeros((RAD, FW + 2 * PAD, CH), BF16)

    @pl.when(c == 0)
    def _():
        ext[:, 0:PAD] = jnp.zeros((FH + 2 * RAD, PAD, CH), BF16)

    @pl.when(c == NCOLS - 1)
    def _():
        ext[:, PAD + FW :] = jnp.zeros((FH + 2 * RAD, PAD, CH), BF16)

    barrier = pltpu.get_barrier_semaphore()
    for device in everyone:
        pl.semaphore_signal(barrier, inc=1, device_id=device, device_id_type=MESH)
    pl.semaphore_wait(barrier, len(everyone))

    def ring(way, d, h, source):
        return pltpu.make_async_remote_copy(
            src_ref=source, dst_ref=kb.at[jnp.minimum(1 + 2 * d + way, 7), h],
            send_sem=ring_send.at[way, d, h], recv_sem=ring_recv.at[way, d, h],
            device_id=ring_to[way], device_id_type=MESH,
        )

    for h in range(NH):
        for way in range(2):
            ring(way, 0, h, c2.at[h]).start()

    def share(j, source, target, send, recv):
        return pltpu.make_async_remote_copy(
            src_ref=source, dst_ref=target, send_sem=send.at[j - 1], recv_sem=recv.at[j - 1],
            device_id=partner(j), device_id_type=MESH,
        )

    lives = [share(j, lv.at[0], lv.at[j], lv_send, lv_recv) for j in (1, 2, 3)]
    asks = [share(1, c1, qb.at[1], q_send, q_recv), share(2, c1, qb.at[2], q_send, q_recv)]
    asks.append(
        pltpu.make_async_remote_copy(
            src_ref=qb.at[2], dst_ref=qb.at[3], send_sem=q_send.at[2], recv_sem=q_recv.at[2],
            device_id=partner(1), device_id_type=MESH,
        )
    )
    asks[1].start()
    asks[0].start()

    own_sel.wait()
    own_cnt.wait()
    slot = lax.broadcasted_iota(jnp.int32, (12, 1, NCOLS), 0)
    chosen = jnp.where(slot < cntv[...].reshape(1, 1, 1), selv[...], 0)
    live = jnp.sum(chosen.astype(F32), axis=0)
    lv[0] = jnp.broadcast_to(jnp.concatenate([live, jnp.zeros((1, 128 - NCOLS), F32)], axis=1), (8, 128))

    for copy in lives:
        copy.start()

    halos = []
    for i, (dy, dx) in enumerate(NEIGHBOURS):
        ys, yn, yt = spans(dy, FH, RAD)
        xs, xn, xt = spans(dx, FW, PAD)
        halos.append(
            pltpu.make_async_remote_copy(
                src_ref=f2.at[ys : ys + yn, xs : xs + xn], dst_ref=ext.at[yt : yt + yn, xt : xt + xn],
                send_sem=halo_send.at[i], recv_sem=halo_recv.at[i],
                device_id=neighbour(dy, dx), device_id_type=MESH,
            )
        )
    each(halos, "start")

    key = lax.broadcasted_iota(jnp.int32, (512, 128), 0)
    query = lax.broadcasted_iota(jnp.int32, (512, 128), 1)
    off_y = key // 32 - RAD - (7 - query // 16)
    off_x = key % 32 - PAD - query % 16
    inside = (jnp.abs(off_y) <= RAD) & (jnp.abs(off_x) <= RAD)
    maskb[...] = jnp.where(inside, 0.0, LOW)

    for j in range(4):
        acc[j, 0] = jnp.full((8, 512), LOW, F32)
        for s in (1, 2, 3):
            acc[j, s] = jnp.zeros((8, 512), F32)

    def set_bias(j):
        lane = lax.broadcasted_iota(jnp.int32, (NCOLS, 128), 1)
        panel = lax.broadcasted_iota(jnp.int32, (NCOLS, 128), 0)
        column = jnp.sum(jnp.where(lane == panel, lv[j][0:1, :], 0.0), axis=1, keepdims=True)
        biasb[j] = jnp.broadcast_to((1.0 - column) * (2.0 * LOW), (NCOLS, 256))

    def split(j):
        q = qb[j].reshape(BH * BW, CH).astype(F32) * SCALE
        high = q.astype(BF16)
        q2[j] = jnp.concatenate([high, (q - high.astype(F32)).astype(BF16)], axis=1)

    def match(at, panel, tiles):
        keys = kb[at].reshape(BH * BW, CH)
        keys = jnp.concatenate([keys, keys], axis=1)
        base = (panel * BW).astype(F32)
        for j in tiles:
            for lanes in (pl.ds(0, 256), pl.ds(256, 256)):
                score = lax.dot_general(keys, q2[j, lanes, :], NT, preferred_element_type=F32)
                score = score.reshape(64, 8, 256)
                top = jnp.max(score, axis=0)
                level = [jnp.exp2(score[i] - top) for i in range(64)]
                odd = []
                while len(level) > 1:
                    odd.append(functools.reduce(jnp.add, level[1::2]))
                    level = [a + b for a, b in zip(level[0::2], level[1::2])]
                total = level[0]
                in_col = 8.0 * (odd[0] + 2.0 * odd[1] + 4.0 * odd[2]) + base * total
                in_row = odd[3] + 2.0 * odd[4] + 4.0 * odd[5]
                seen = top + biasb[j, pl.ds(panel, 1), :]
                before = acc[j, 0, :, lanes]
                now = jnp.maximum(before, seen)
                keep = jnp.exp2(before - now)
                take = jnp.exp2(seen - now)
                acc[j, 0, :, lanes] = now
                acc[j, 1, :, lanes] = keep * acc[j, 1, :, lanes] + take * total
                acc[j, 2, :, lanes] = keep * acc[j, 2, :, lanes] + take * in_col
                acc[j, 3, :, lanes] = keep * acc[j, 3, :, lanes] + take * in_row

    def window(b):
        by, bx = b // 8, b % 8
        rows = pl.ds(by * 8, 16)
        keys = ext[rows, pl.ds(pl.multiple_of(bx * 16, 16), 32), :].reshape(512, CH)
        queries = f1v[pl.ds(by * 8, 8), pl.ds(pl.multiple_of(bx * 16, 16), 16), :]
        queries = jnp.concatenate([queries[7 - i] for i in range(8)], axis=0)
        score = lax.dot_general(keys, queries, NT, preferred_element_type=F32) + maskb[...]
        top = jnp.max(score, axis=0, keepdims=True)
        weight = jnp.exp2((score - top) * SCALE)
        total = jnp.sum(weight, axis=0, keepdims=True)
        pairs = weight.reshape(8, 2, 32, 128)
        pairs = (pairs[:, 0] + pairs[:, 1]) * (1.0 / total)
        pscr[...] = pairs.reshape(256, 128)
        wbuf[b] = pscr[pl.ds(0, 128, stride=2), :] + pscr[pl.ds(1, 128, stride=2), :]

    def two_windows(i, _):
        window(2 * i)
        window(2 * i + 1)
        return 0

    def panel_of(p):
        depth = (p + 1) // 2
        sign = jnp.where(p == 7, -1, 1 - 2 * (p % 2))
        return ylo * 16 + ((z + NZ + sign * depth) % NZ) * 2 + core

    def forward(n):
        d = n // 2
        for i in range(NH // 2):
            h = (n % 2) * (NH // 2) + i
            for way in range(2):
                ring(way, d, h, kb.at[0, 0]).wait_recv()

                @pl.when((d < 2) | (n % 2 == way))
                def _(way=way, h=h):
                    ring(way, d + 1, h, kb.at[1 + 2 * d + way, h]).start()

    set_bias(0)
    own_q.wait()
    split(0)
    own_k.wait()
    match(0, panel_of(0), (0,))
    forward(0)
    asks[1].wait_recv()
    asks[2].start()
    forward(1)
    for j in (1, 2, 3):
        lives[j - 1].wait_recv()
        set_bias(j)
        if j != 2:
            asks[j - 1].wait_recv()
        split(j)
    match(0, panel_of(0), (1, 2, 3))

    def step(p, _):
        @pl.when(p < 5)
        def _():
            forward(p + 1)

        match(p, panel_of(p), (0, 1, 2, 3))
        return 0

    lax.fori_loop(1, 7, step, 0)
    for i in range(NH // 2):
        for way in range(2):
            ring(way, 3, way * (NH // 2) + i, kb.at[0, 0]).wait_recv()

    sub = lax.broadcasted_iota(jnp.int32, (8, 512), 0).astype(F32)

    def moments(j):
        top8, total, in_col, in_row = acc[j, 0], acc[j, 1], acc[j, 2], acc[j, 3]
        in_col = in_col + sub * total
        top = jnp.max(top8, axis=0, keepdims=True)
        part = jnp.exp2(top8 - top)
        sums = [jnp.sum(part * v, axis=0, keepdims=True) for v in (total, in_col, in_row)]
        return jnp.concatenate([top] + sums + [jnp.zeros((4, 512), F32)], axis=0)

    backs = [share(j, st_tx.at[j - 1], st_rx.at[j - 1], st_send, st_recv) for j in (1, 2, 3)]
    for j in (3, 2, 1):
        match(7, panel_of(7), (j,))
        st_tx[j - 1] = moments(j)
        backs[j - 1].start()
    match(7, panel_of(7), (0,))
    parts = [moments(0)]
    own_f1.wait()
    own_f2.wait()
    each(halos, "wait_recv")
    lax.fori_loop(0, 4, two_windows, 0)
    for j in (1, 2, 3):
        backs[j - 1].wait_recv()
        parts.append(st_rx[j - 1])
    top = functools.reduce(jnp.maximum, [p[0:1] for p in parts])
    scales = [jnp.exp2(p[0:1] - top) for p in parts]
    total, in_col, in_row = (
        functools.reduce(jnp.add, [s * p[i : i + 1] for s, p in zip(scales, parts)]) for i in (1, 2, 3)
    )
    cell = lax.broadcasted_iota(jnp.int32, (1, 512), 1)
    query_col = (c * BW + cell % BW).astype(F32)
    query_row = (cell // BW).astype(F32)
    flow_x = (in_col / total - query_col) * (1.0 / 256.0)
    flow_y = (in_row / total - query_row) * (1.0 / 256.0)
    flow = jnp.concatenate([f[:, 128 * i : 128 * i + 128] for f in (flow_x, flow_y) for i in range(4)], axis=0)
    fl[1, 1] = flow
    edges = []
    for i, (dy, dx) in enumerate(NEIGHBOURS):
        edges.append(
            pltpu.make_async_remote_copy(
                src_ref=fl.at[1, 1], dst_ref=fl.at[1 - dy, 1 - dx],
                send_sem=fl_send.at[i], recv_sem=fl_recv.at[i],
                device_id=neighbour(dy, dx), device_id_type=MESH,
            )
        )
    each(edges, "start")

    for k in range(2):
        for i in range(4):
            pair = flow[k * 4 + i : k * 4 + i + 1, :]
            coarse_out[k, 2 * i : 2 * i + 1, :] = pair[:, :BW]
            coarse_out[k, 2 * i + 1 : 2 * i + 2, :] = pair[:, BW:]
    lax.fori_loop(4, 8, two_windows, 0)

    def spread(k, e, lo, hi, sources):
        shape = (hi - lo, 128)
        row = (e - 2) % 8
        i72 = lax.broadcasted_iota(jnp.int32, shape, 0) + lo
        lane = lax.broadcasted_iota(jnp.int32, shape, 1)
        goal = jnp.where(i72 < 4, 60 + i72, jnp.where(i72 < 68, i72 - 4, i72 - 68)) + (row % 2) * 64
        at = k * 4 + row // 2
        left, mid, right = (s[at : at + 1, :] for s in sources)
        pick = jnp.where(i72 < 4, left, jnp.where(i72 < 68, mid, right))
        value = jnp.sum(jnp.where(lane == goal, pick, 0.0), axis=1, keepdims=True)
        ft[k, e, lo:hi, :] = jnp.broadcast_to(value, shape)

    def weighed(k, b, rows, lo, hi):
        by, bx = b // 8, b % 8
        weight = wbuf[b].reshape(8, 16, 128)[rows.start : rows.stop, lo:hi]
        value = ft[k, by * 4 + rows.start : by * 4 + rows.stop, bx * 8 + lo : bx * 8 + hi, :]
        terms = (weight * value).reshape(-1, 8, 128)
        return functools.reduce(jnp.add, [terms[i] for i in range(terms.shape[0])])

    def inner(b):
        by, bx = b // 8, b % 8
        return (range(2, 8) if by == 0 else range(0, 6)), (8 if bx == 0 else 0), (8 if bx == 7 else 16)

    for k in range(2):
        for e in range(2, 10):
            spread(k, e, 8, 64, (flow, flow, flow))
        for b in range(16):
            part_sum[k, b] = weighed(k, b, *inner(b))

    each(edges, "wait_recv")
    for k in range(2):
        for e in range(12):
            sources = [fl[0 if e < 2 else (1 if e < 10 else 2), tx] for tx in range(3)]
            if 2 <= e < 10:
                spread(k, e, 0, 8, sources)
                spread(k, e, 64, 72, sources)
            else:
                spread(k, e, 0, 72, sources)
    lane8 = lax.broadcasted_iota(jnp.int32, (8, 128), 1)
    sub8 = lax.broadcasted_iota(jnp.int32, (8, 128), 0)
    for k in range(2):
        for by in range(2):
            band = jnp.zeros((8, 128), F32)
            for bx in range(8):
                b = by * 8 + bx
                rows, lo, hi = inner(b)
                value = part_sum[k, b] + weighed(k, b, range(0, 2) if by == 0 else range(6, 8), 0, 16)
                if lo:
                    value = value + weighed(k, b, rows, 0, lo)
                if hi < 16:
                    value = value + weighed(k, b, rows, hi, 16)
                value = jnp.broadcast_to(jnp.sum(value, axis=0, keepdims=True), (8, 128))
                value = pltpu.roll(value, (bx * 16 + 16) % 128, 1)
                band = jnp.where((lane8 // 16 + sub8) % 8 == bx, value, band)
            fine_out[k, by * 8 : by * 8 + 8, :] = pltpu.roll(band, 0, 1, stride=16, stride_axis=0)

    for h in range(NH):
        for way in range(2):
            for d in range(4):
                if d < 3 or h // (NH // 2) == way:
                    ring(way, d, h, kb.at[0, 0]).wait_send()
    for copy in asks + lives + backs:
        copy.wait_send()
    each(halos, "wait_send")
    each(edges, "wait_send")


def local(coarse_one, coarse_two, fine_one, fine_two, selection, counts):
    vm = pltpu.VMEM
    dma = pltpu.SemaphoreType.DMA
    any_spec = pl.BlockSpec(memory_space=pl.ANY)
    vm_spec = pl.BlockSpec(memory_space=pltpu.VMEM)
    coarse, fine = pl.pallas_call(
        kernel,
        out_shape=(jax.ShapeDtypeStruct((2, BH, BW), F32), jax.ShapeDtypeStruct((2, FH, FW), F32)),
        in_specs=[any_spec] * 5 + [pl.BlockSpec(memory_space=pltpu.HBM)],
        out_specs=(vm_spec, vm_spec),
        scratch_shapes=[
            vm((8, NH, BH // NH, BW, CH), BF16),
            vm((4, 2, 4, BW, CH), BF16),
            vm((4, BH * BW, 2 * CH), BF16),
            vm((FH, FW, CH), BF16),
            vm((FH + 2 * RAD, FW + 2 * PAD, CH), BF16),
            vm((16, 128, 128), F32),
            vm((512, 128), F32),
            vm((256, 128), F32),
            vm((12, 1, NCOLS), jnp.int32),
            vm((1, 1), jnp.int32),
            vm((4, 8, 128), F32),
            vm((4, NCOLS, 256), F32),
            vm((4, 4, 8, 512), F32),
            vm((3, 8, 512), F32),
            vm((3, 8, 512), F32),
            vm((3, 3, 8, 128), F32),
            vm((2, 12, 72, 128), F32),
            vm((2, 16, 8, 128), F32),
            dma((2, 4, NH)), dma((2, 4, NH)),
            dma((3,)), dma((3,)), dma((3,)), dma((3,)),
            dma((8,)), dma((8,)),
            dma((3,)), dma((3,)),
            dma((8,)), dma((8,)),
            dma((6,)),
        ],
        compiler_params=pltpu.CompilerParams(collective_id=0, has_side_effects=True, vmem_limit_bytes=63 << 20),
        name="flow",
    )(
        coarse_one.reshape(2, 4, BW, CH), coarse_two.reshape(NH, BH // NH, BW, CH), fine_one, fine_two,
        selection.reshape(12, 1, NCOLS), counts
    )
    return coarse, fine


def solution(mesh):
    return jax.shard_map(
        local,
        mesh=mesh,
        in_specs=(
            P("rows", "cols", None),
            P("rows", "cols", None),
            P("rows", "cols", None),
            P("rows", "cols", None),
            P("rows", "cols", None, None),
            P("rows", "cols"),
        ),
        out_specs=(P(None, "rows", "cols"), P(None, "rows", "cols")),
        check_vma=False,
    )
```

```python
import functools

import jax
import jax.numpy as jnp
import numpy as np
from jax import lax
from jax.experimental import pallas as pl
from jax.experimental.pallas import tpu as pltpu
from jax.sharding import PartitionSpec as P

MESH = pl.DeviceIdType.MESH
F32 = jnp.float32
BF16 = jnp.bfloat16
NROWS, NCOLS = 8, 32
NZ = 8
NH = 2
CH = 128
BH, BW = 8, 64
FH, FW = 16, 128
RAD = 4
PAD = 8
SCALE = float(np.log2(np.e) / np.sqrt(128.0))
LOW = -1.0e30
NEIGHBOURS = [(dy, dx) for dy in (-1, 0, 1) for dx in (-1, 0, 1) if (dy, dx) != (0, 0)]
NT = (((1,), (1,)), ((), ()))


def spans(d, size, halo):
    if d == 0:
        return 0, size, halo
    if d == 1:
        return size - halo, halo, 0
    return 0, halo, size + halo


def kernel(
    c1, c2, f1, f2, sel, cnt,
    coarse_out, fine_out,
    kb, qb, q2, f1v, ext, wbuf, maskb, pscr, selv, cntv, lv, biasb, acc, st_tx, st_rx, fl, ft, part_sum,
    ring_send, ring_recv, q_send, q_recv, lv_send, lv_recv, halo_send, halo_recv,
    st_send, st_recv, fl_send, fl_recv, loc,
):
    r = lax.axis_index("rows")
    c = lax.axis_index("cols")
    ylo = c // 16
    z = (c // 2) % NZ
    core = c % 2

    def at_z(zz):
        return (r, ylo * 16 + zz * 2 + core)

    ring_to = (at_z((z + 1) % NZ), at_z((z + NZ - 1) % NZ))

    def partner(j):
        return (r, ((ylo + j // 2) % 2) * 16 + z * 2 + (core + j % 2) % 2)

    def neighbour(dy, dx):
        return ((r + dy + NROWS) % NROWS, (c + dx + NCOLS) % NCOLS)

    def exists(dy, dx):
        there = True
        for d, at, last in ((dy, r, NROWS - 1), (dx, c, NCOLS - 1)):
            if d == -1:
                there = there & (at > 0)
            if d == 1:
                there = there & (at < last)
        return there

    def each(copies, what):
        for copy, (dy, dx) in zip(copies, NEIGHBOURS):
            there = exists(-dy, -dx) if what == "wait_recv" else exists(dy, dx)

            @pl.when(there)
            def _(copy=copy):
                getattr(copy, what)()

    everyone = list(ring_to) + [partner(j) for j in (1, 2, 3)] + [neighbour(*n) for n in NEIGHBOURS]

    fl[...] = jnp.zeros((3, 3, 8, 128), F32)

    @pl.when(r == 0)
    def _():
        ext[0:RAD] = jnp.zeros((RAD, FW + 2 * PAD, CH), BF16)

    @pl.when(r == NROWS - 1)
    def _():
        ext[RAD + FH :] = jnp.zeros((RAD, FW + 2 * PAD, CH), BF16)

    @pl.when(c == 0)
    def _():
        ext[:, 0:PAD] = jnp.zeros((FH + 2 * RAD, PAD, CH), BF16)

    @pl.when(c == NCOLS - 1)
    def _():
        ext[:, PAD + FW :] = jnp.zeros((FH + 2 * RAD, PAD, CH), BF16)

    barrier = pltpu.get_barrier_semaphore()
    for device in everyone:
        pl.semaphore_signal(barrier, inc=1, device_id=device, device_id_type=MESH)
    own_sel = pltpu.make_async_copy(sel, selv, loc.at[4])
    own_cnt = pltpu.make_async_copy(cnt, cntv, loc.at[5])
    own_k = pltpu.make_async_copy(c2, kb.at[0], loc.at[0])
    own_q = pltpu.make_async_copy(c1, qb.at[0], loc.at[1])
    own_f1 = pltpu.make_async_copy(f1, f1v, loc.at[2])
    own_f2 = pltpu.make_async_copy(f2, ext.at[RAD : RAD + FH, PAD : PAD + FW], loc.at[3])
    for copy in (own_sel, own_cnt, own_k, own_q, own_f1, own_f2):
        copy.start()

    pl.semaphore_wait(barrier, len(everyone))

    def ring(way, d, h, source):
        return pltpu.make_async_remote_copy(
            src_ref=source, dst_ref=kb.at[jnp.minimum(1 + 2 * d + way, 7), h],
            send_sem=ring_send.at[way, d, h], recv_sem=ring_recv.at[way, d, h],
            device_id=ring_to[way], device_id_type=MESH,
        )

    for h in range(NH):
        for way in range(2):
            ring(way, 0, h, c2.at[h]).start()

    def share(j, source, target, send, recv):
        return pltpu.make_async_remote_copy(
            src_ref=source, dst_ref=target, send_sem=send.at[j - 1], recv_sem=recv.at[j - 1],
            device_id=partner(j), device_id_type=MESH,
        )

    lives = [share(j, lv.at[0], lv.at[j], lv_send, lv_recv) for j in (1, 2, 3)]
    asks = [share(1, c1, qb.at[1], q_send, q_recv), share(2, c1, qb.at[2], q_send, q_recv)]
    asks.append(
        pltpu.make_async_remote_copy(
            src_ref=qb.at[2], dst_ref=qb.at[3], send_sem=q_send.at[2], recv_sem=q_recv.at[2],
            device_id=partner(1), device_id_type=MESH,
        )
    )
    asks[1].start()
    asks[0].start()

    own_sel.wait()
    own_cnt.wait()
    slot = lax.broadcasted_iota(jnp.int32, (12, 1, NCOLS), 0)
    chosen = jnp.where(slot < cntv[...].reshape(1, 1, 1), selv[...], 0)
    live = jnp.sum(chosen.astype(F32), axis=0)
    lv[0] = jnp.broadcast_to(jnp.concatenate([live, jnp.zeros((1, 128 - NCOLS), F32)], axis=1), (8, 128))

    for copy in lives:
        copy.start()

    halos = []
    for i, (dy, dx) in enumerate(NEIGHBOURS):
        ys, yn, yt = spans(dy, FH, RAD)
        xs, xn, xt = spans(dx, FW, PAD)
        halos.append(
            pltpu.make_async_remote_copy(
                src_ref=f2.at[ys : ys + yn, xs : xs + xn], dst_ref=ext.at[yt : yt + yn, xt : xt + xn],
                send_sem=halo_send.at[i], recv_sem=halo_recv.at[i],
                device_id=neighbour(dy, dx), device_id_type=MESH,
            )
        )

    key = lax.broadcasted_iota(jnp.int32, (512, 128), 0)
    query = lax.broadcasted_iota(jnp.int32, (512, 128), 1)
    off_y = key // 32 - RAD - (7 - query // 16)
    off_x = key % 32 - PAD - query % 16
    inside = (jnp.abs(off_y) <= RAD) & (jnp.abs(off_x) <= RAD)
    maskb[...] = jnp.where(inside, 0.0, LOW)

    for j in range(4):
        acc[j, 0] = jnp.full((8, 512), LOW, F32)
        for s in (1, 2, 3):
            acc[j, s] = jnp.zeros((8, 512), F32)

    def set_bias(j):
        lane = lax.broadcasted_iota(jnp.int32, (NCOLS, 128), 1)
        panel = lax.broadcasted_iota(jnp.int32, (NCOLS, 128), 0)
        column = jnp.sum(jnp.where(lane == panel, lv[j][0:1, :], 0.0), axis=1, keepdims=True)
        biasb[j] = jnp.broadcast_to((1.0 - column) * (2.0 * LOW), (NCOLS, 256))

    def split(j):
        q = qb[j].reshape(BH * BW, CH).astype(F32) * SCALE
        high = q.astype(BF16)
        q2[j] = jnp.concatenate([high, (q - high.astype(F32)).astype(BF16)], axis=1)

    def match(at, panel, tiles):
        keys = kb[at].reshape(BH * BW, CH)
        keys = jnp.concatenate([keys, keys], axis=1)
        base = (panel * BW).astype(F32)
        for j in tiles:
            for lanes in (pl.ds(0, 256), pl.ds(256, 256)):
                score = lax.dot_general(keys, q2[j, lanes, :], NT, preferred_element_type=F32)
                score = score.reshape(64, 8, 256)
                top = jnp.max(score, axis=0)
                level = [jnp.exp2(score[i] - top) for i in range(64)]
                odd = []
                while len(level) > 1:
                    odd.append(functools.reduce(jnp.add, level[1::2]))
                    level = [a + b for a, b in zip(level[0::2], level[1::2])]
                total = level[0]
                in_col = 8.0 * (odd[0] + 2.0 * odd[1] + 4.0 * odd[2]) + base * total
                in_row = odd[3] + 2.0 * odd[4] + 4.0 * odd[5]
                seen = top + biasb[j, pl.ds(panel, 1), :]
                before = acc[j, 0, :, lanes]
                now = jnp.maximum(before, seen)
                keep = jnp.exp2(before - now)
                take = jnp.exp2(seen - now)
                acc[j, 0, :, lanes] = now
                acc[j, 1, :, lanes] = keep * acc[j, 1, :, lanes] + take * total
                acc[j, 2, :, lanes] = keep * acc[j, 2, :, lanes] + take * in_col
                acc[j, 3, :, lanes] = keep * acc[j, 3, :, lanes] + take * in_row

    def window(b):
        by, bx = b // 8, b % 8
        rows = pl.ds(by * 8, 16)
        keys = ext[rows, pl.ds(pl.multiple_of(bx * 16, 16), 32), :].reshape(512, CH)
        queries = f1v[pl.ds(by * 8, 8), pl.ds(pl.multiple_of(bx * 16, 16), 16), :]
        queries = jnp.concatenate([queries[7 - i] for i in range(8)], axis=0)
        score = lax.dot_general(keys, queries, NT, preferred_element_type=F32) + maskb[...]
        top = jnp.max(score, axis=0, keepdims=True)
        weight = jnp.exp2((score - top) * SCALE)
        total = jnp.sum(weight, axis=0, keepdims=True)
        pairs = weight.reshape(8, 2, 32, 128)
        pairs = (pairs[:, 0] + pairs[:, 1]) * (1.0 / total)
        pscr[...] = pairs.reshape(256, 128)
        wbuf[b] = pscr[pl.ds(0, 128, stride=2), :] + pscr[pl.ds(1, 128, stride=2), :]

    def two_windows(i, _):
        window(2 * i)
        window(2 * i + 1)
        return 0

    def panel_of(p):
        depth = (p + 1) // 2
        sign = jnp.where(p == 7, -1, 1 - 2 * (p % 2))
        return ylo * 16 + ((z + NZ + sign * depth) % NZ) * 2 + core

    def forward(n):
        d = n // 2
        for i in range(NH // 2):
            h = (n % 2) * (NH // 2) + i
            for way in range(2):
                ring(way, d, h, kb.at[0, 0]).wait_recv()

                @pl.when((d < 2) | (n % 2 == way))
                def _(way=way, h=h):
                    ring(way, d + 1, h, kb.at[1 + 2 * d + way, h]).start()

    set_bias(0)
    own_q.wait()
    split(0)
    own_k.wait()
    match(0, panel_of(0), (0,))
    forward(0)
    asks[1].wait_recv()
    asks[2].start()
    forward(1)
    each(halos, "start")
    for j in (1, 2, 3):
        lives[j - 1].wait_recv()
        set_bias(j)
        if j != 2:
            asks[j - 1].wait_recv()
        split(j)
        match(0, panel_of(0), (j,))

    def step(p, _):
        @pl.when(p < 5)
        def _():
            forward(p + 1)

        match(p, panel_of(p), (0, 1, 2, 3))
        return 0

    lax.fori_loop(1, 7, step, 0)
    for i in range(NH // 2):
        for way in range(2):
            ring(way, 3, way * (NH // 2) + i, kb.at[0, 0]).wait_recv()

    sub = lax.broadcasted_iota(jnp.int32, (8, 512), 0).astype(F32)

    def moments(j):
        top8, total, in_col, in_row = acc[j, 0], acc[j, 1], acc[j, 2], acc[j, 3]
        in_col = in_col + sub * total
        top = jnp.max(top8, axis=0, keepdims=True)
        part = jnp.exp2(top8 - top)
        sums = [jnp.sum(part * v, axis=0, keepdims=True) for v in (total, in_col, in_row)]
        return jnp.concatenate([top] + sums + [jnp.zeros((4, 512), F32)], axis=0)

    backs = [share(j, st_tx.at[j - 1], st_rx.at[j - 1], st_send, st_recv) for j in (1, 2, 3)]
    for j in (3, 2, 1):
        match(7, panel_of(7), (j,))
        st_tx[j - 1] = moments(j)
        backs[j - 1].start()
    match(7, panel_of(7), (0,))
    parts = [moments(0)]
    own_f1.wait()
    own_f2.wait()
    each(halos, "wait_recv")
    lax.fori_loop(0, 4, two_windows, 0)
    for j in (1, 2, 3):
        backs[j - 1].wait_recv()
        parts.append(st_rx[j - 1])
    top = functools.reduce(jnp.maximum, [p[0:1] for p in parts])
    scales = [jnp.exp2(p[0:1] - top) for p in parts]
    total, in_col, in_row = (
        functools.reduce(jnp.add, [s * p[i : i + 1] for s, p in zip(scales, parts)]) for i in (1, 2, 3)
    )
    cell = lax.broadcasted_iota(jnp.int32, (1, 512), 1)
    query_col = (c * BW + cell % BW).astype(F32)
    query_row = (cell // BW).astype(F32)
    flow_x = (in_col / total - query_col) * (1.0 / 256.0)
    flow_y = (in_row / total - query_row) * (1.0 / 256.0)
    flow = jnp.concatenate([f[:, 128 * i : 128 * i + 128] for f in (flow_x, flow_y) for i in range(4)], axis=0)
    fl[1, 1] = flow
    edges = []
    for i, (dy, dx) in enumerate(NEIGHBOURS):
        edges.append(
            pltpu.make_async_remote_copy(
                src_ref=fl.at[1, 1], dst_ref=fl.at[1 - dy, 1 - dx],
                send_sem=fl_send.at[i], recv_sem=fl_recv.at[i],
                device_id=neighbour(dy, dx), device_id_type=MESH,
            )
        )
    each(edges, "start")

    for k in range(2):
        for i in range(4):
            pair = flow[k * 4 + i : k * 4 + i + 1, :]
            coarse_out[k, 2 * i : 2 * i + 1, :] = pair[:, :BW]
            coarse_out[k, 2 * i + 1 : 2 * i + 2, :] = pair[:, BW:]
    lax.fori_loop(4, 8, two_windows, 0)

    def spread(k, e, lo, hi, sources):
        shape = (hi - lo, 128)
        row = (e - 2) % 8
        i72 = lax.broadcasted_iota(jnp.int32, shape, 0) + lo
        lane = lax.broadcasted_iota(jnp.int32, shape, 1)
        goal = jnp.where(i72 < 4, 60 + i72, jnp.where(i72 < 68, i72 - 4, i72 - 68)) + (row % 2) * 64
        at = k * 4 + row // 2
        left, mid, right = (s[at : at + 1, :] for s in sources)
        pick = jnp.where(i72 < 4, left, jnp.where(i72 < 68, mid, right))
        value = jnp.sum(jnp.where(lane == goal, pick, 0.0), axis=1, keepdims=True)
        ft[k, e, lo:hi, :] = jnp.broadcast_to(value, shape)

    def weighed(k, b, rows, lo, hi):
        by, bx = b // 8, b % 8
        weight = wbuf[b].reshape(8, 16, 128)[rows.start : rows.stop, lo:hi]
        value = ft[k, by * 4 + rows.start : by * 4 + rows.stop, bx * 8 + lo : bx * 8 + hi, :]
        terms = (weight * value).reshape(-1, 8, 128)
        return functools.reduce(jnp.add, [terms[i] for i in range(terms.shape[0])])

    def inner(b):
        by, bx = b // 8, b % 8
        return (range(2, 8) if by == 0 else range(0, 6)), (8 if bx == 0 else 0), (8 if bx == 7 else 16)

    for k in range(2):
        for e in range(2, 10):
            spread(k, e, 8, 64, (flow, flow, flow))
        for b in range(16):
            part_sum[k, b] = weighed(k, b, *inner(b))

    each(edges, "wait_recv")
    for k in range(2):
        for e in range(12):
            sources = [fl[0 if e < 2 else (1 if e < 10 else 2), tx] for tx in range(3)]
            if 2 <= e < 10:
                spread(k, e, 0, 8, sources)
                spread(k, e, 64, 72, sources)
            else:
                spread(k, e, 0, 72, sources)
    lane8 = lax.broadcasted_iota(jnp.int32, (8, 128), 1)
    sub8 = lax.broadcasted_iota(jnp.int32, (8, 128), 0)
    for k in range(2):
        for by in range(2):
            band = jnp.zeros((8, 128), F32)
            for bx in range(8):
                b = by * 8 + bx
                rows, lo, hi = inner(b)
                value = part_sum[k, b] + weighed(k, b, range(0, 2) if by == 0 else range(6, 8), 0, 16)
                if lo:
                    value = value + weighed(k, b, rows, 0, lo)
                if hi < 16:
                    value = value + weighed(k, b, rows, hi, 16)
                value = jnp.broadcast_to(jnp.sum(value, axis=0, keepdims=True), (8, 128))
                value = pltpu.roll(value, (bx * 16 + 16) % 128, 1)
                band = jnp.where((lane8 // 16 + sub8) % 8 == bx, value, band)
            fine_out[k, by * 8 : by * 8 + 8, :] = pltpu.roll(band, 0, 1, stride=16, stride_axis=0)

    for h in range(NH):
        for way in range(2):
            for d in range(4):
                if d < 3 or h // (NH // 2) == way:
                    ring(way, d, h, kb.at[0, 0]).wait_send()
    for copy in asks + lives + backs:
        copy.wait_send()
    each(halos, "wait_send")
    each(edges, "wait_send")


def local(coarse_one, coarse_two, fine_one, fine_two, selection, counts):
    vm = pltpu.VMEM
    dma = pltpu.SemaphoreType.DMA
    any_spec = pl.BlockSpec(memory_space=pl.ANY)
    vm_spec = pl.BlockSpec(memory_space=pltpu.VMEM)
    coarse, fine = pl.pallas_call(
        kernel,
        out_shape=(jax.ShapeDtypeStruct((2, BH, BW), F32), jax.ShapeDtypeStruct((2, FH, FW), F32)),
        in_specs=[any_spec] * 5 + [pl.BlockSpec(memory_space=pltpu.HBM)],
        out_specs=(vm_spec, vm_spec),
        scratch_shapes=[
            vm((8, NH, BH // NH, BW, CH), BF16),
            vm((4, 2, 4, BW, CH), BF16),
            vm((4, BH * BW, 2 * CH), BF16),
            vm((FH, FW, CH), BF16),
            vm((FH + 2 * RAD, FW + 2 * PAD, CH), BF16),
            vm((16, 128, 128), F32),
            vm((512, 128), F32),
            vm((256, 128), F32),
            vm((12, 1, NCOLS), jnp.int32),
            vm((1, 1), jnp.int32),
            vm((4, 8, 128), F32),
            vm((4, NCOLS, 256), F32),
            vm((4, 4, 8, 512), F32),
            vm((3, 8, 512), F32),
            vm((3, 8, 512), F32),
            vm((3, 3, 8, 128), F32),
            vm((2, 12, 72, 128), F32),
            vm((2, 16, 8, 128), F32),
            dma((2, 4, NH)), dma((2, 4, NH)),
            dma((3,)), dma((3,)), dma((3,)), dma((3,)),
            dma((8,)), dma((8,)),
            dma((3,)), dma((3,)),
            dma((8,)), dma((8,)),
            dma((6,)),
        ],
        compiler_params=pltpu.CompilerParams(collective_id=0, has_side_effects=True, vmem_limit_bytes=55136 << 10),
        name="flow",
    )(
        coarse_one.reshape(2, 4, BW, CH), coarse_two.reshape(NH, BH // NH, BW, CH), fine_one, fine_two,
        selection.reshape(12, 1, NCOLS), counts
    )
    return coarse, fine


def solution(mesh):
    return jax.shard_map(
        local,
        mesh=mesh,
        in_specs=(
            P("rows", "cols", None),
            P("rows", "cols", None),
            P("rows", "cols", None),
            P("rows", "cols", None),
            P("rows", "cols", None, None),
            P("rows", "cols"),
        ),
        out_specs=(P(None, "rows", "cols"), P(None, "rows", "cols")),
        check_vma=False,
    )
```

```python
import functools

import jax
import jax.numpy as jnp
import numpy as np
from jax import lax
from jax.experimental import pallas as pl
from jax.experimental.pallas import tpu as pltpu
from jax.sharding import PartitionSpec as P

MESH = pl.DeviceIdType.MESH
F32 = jnp.float32
BF16 = jnp.bfloat16
NROWS, NCOLS = 8, 32
NZ = 8
GROUP = 4
NH = 4
CH = 128
BH, BW = 8, 64
FH, FW = 16, 128
RAD = 4
PAD = 8
SCALE = float(np.log2(np.e) / np.sqrt(128.0))
LOW = -1.0e30
NEIGHBOURS = [(dy, dx) for dy in (-1, 0, 1) for dx in (-1, 0, 1) if (dy, dx) != (0, 0)]
NT = (((1,), (1,)), ((), ()))


def spans(d, size, halo):
    if d == 0:
        return 0, size, halo
    if d == 1:
        return size - halo, halo, 0
    return 0, halo, size + halo


def kernel(
    c1, c2, f1, f2, sel, cnt,
    coarse_out, fine_out,
    kb, qb, q2, f1v, ext, wbuf, maskb, pscr, selv, cntv, lv, biasb, acc, st_tx, st_rx, fl, ft, part_sum,
    ring_send, ring_recv, q_send, q_recv, lv_send, lv_recv, halo_send, halo_recv,
    st_send, st_recv, fl_send, fl_recv, loc,
):
    r = lax.axis_index("rows")
    c = lax.axis_index("cols")
    ylo = c // 16
    z = (c // 2) % NZ
    core = c % 2

    def at_z(zz):
        return (r, ylo * 16 + zz * 2 + core)

    ring_to = (at_z((z + 1) % NZ), at_z((z + NZ - 1) % NZ))

    def partner(j):
        return (r, ((ylo + j // 2) % 2) * 16 + z * 2 + (core + j % 2) % 2)

    def neighbour(dy, dx):
        return ((r + dy + NROWS) % NROWS, (c + dx + NCOLS) % NCOLS)

    def exists(dy, dx):
        there = True
        for d, at, last in ((dy, r, NROWS - 1), (dx, c, NCOLS - 1)):
            if d == -1:
                there = there & (at > 0)
            if d == 1:
                there = there & (at < last)
        return there

    def each(copies, what):
        for copy, (dy, dx) in zip(copies, NEIGHBOURS):
            there = exists(-dy, -dx) if what == "wait_recv" else exists(dy, dx)

            @pl.when(there)
            def _(copy=copy):
                getattr(copy, what)()

    everyone = list(ring_to) + [partner(j) for j in (1, 2, 3)] + [neighbour(*n) for n in NEIGHBOURS]

    fl[...] = jnp.zeros((3, 3, 8, 128), F32)

    @pl.when(r == 0)
    def _():
        ext[0:RAD] = jnp.zeros((RAD, FW + 2 * PAD, CH), BF16)

    @pl.when(r == NROWS - 1)
    def _():
        ext[RAD + FH :] = jnp.zeros((RAD, FW + 2 * PAD, CH), BF16)

    @pl.when(c == 0)
    def _():
        ext[:, 0:PAD] = jnp.zeros((FH + 2 * RAD, PAD, CH), BF16)

    @pl.when(c == NCOLS - 1)
    def _():
        ext[:, PAD + FW :] = jnp.zeros((FH + 2 * RAD, PAD, CH), BF16)

    barrier = pltpu.get_barrier_semaphore()
    for device in everyone:
        pl.semaphore_signal(barrier, inc=1, device_id=device, device_id_type=MESH)
    own_sel = pltpu.make_async_copy(sel, selv, loc.at[4])
    own_cnt = pltpu.make_async_copy(cnt, cntv, loc.at[5])
    own_k = pltpu.make_async_copy(c2, kb.at[0], loc.at[0])
    own_q = pltpu.make_async_copy(c1, qb.at[0], loc.at[1])
    own_f1 = pltpu.make_async_copy(f1, f1v, loc.at[2])
    own_f2 = pltpu.make_async_copy(f2, ext.at[RAD : RAD + FH, PAD : PAD + FW], loc.at[3])
    for copy in (own_sel, own_cnt, own_k, own_q, own_f1, own_f2):
        copy.start()

    pl.semaphore_wait(barrier, len(everyone))

    def ring(way, d, h, source):
        return pltpu.make_async_remote_copy(
            src_ref=source, dst_ref=kb.at[jnp.minimum(1 + 2 * d + way, 7), h],
            send_sem=ring_send.at[way, d, h], recv_sem=ring_recv.at[way, d, h],
            device_id=ring_to[way], device_id_type=MESH,
        )

    for h in range(NH // 2):
        for way in range(2):
            ring(way, 0, h, c2.at[h]).start()

    def share(j, source, target, send, recv):
        return pltpu.make_async_remote_copy(
            src_ref=source, dst_ref=target, send_sem=send.at[j - 1], recv_sem=recv.at[j - 1],
            device_id=partner(j), device_id_type=MESH,
        )

    lives = [share(j, lv.at[0], lv.at[j], lv_send, lv_recv) for j in (1, 2, 3)]
    asks = [share(1, c1, qb.at[1], q_send, q_recv), share(2, c1, qb.at[2], q_send, q_recv)]
    asks.append(
        pltpu.make_async_remote_copy(
            src_ref=qb.at[2], dst_ref=qb.at[3], send_sem=q_send.at[2], recv_sem=q_recv.at[2],
            device_id=partner(1), device_id_type=MESH,
        )
    )
    asks[1].start()
    asks[0].start()

    own_sel.wait()
    own_cnt.wait()
    slot = lax.broadcasted_iota(jnp.int32, (12, 1, NCOLS), 0)
    chosen = jnp.where(slot < cntv[...].reshape(1, 1, 1), selv[...], 0)
    live = jnp.sum(chosen.astype(F32), axis=0)
    lv[0] = jnp.broadcast_to(jnp.concatenate([live, jnp.zeros((1, 128 - NCOLS), F32)], axis=1), (8, 128))

    for copy in lives:
        copy.start()

    halos = []
    for i, (dy, dx) in enumerate(NEIGHBOURS):
        ys, yn, yt = spans(dy, FH, RAD)
        xs, xn, xt = spans(dx, FW, PAD)
        halos.append(
            pltpu.make_async_remote_copy(
                src_ref=f2.at[ys : ys + yn, xs : xs + xn], dst_ref=ext.at[yt : yt + yn, xt : xt + xn],
                send_sem=halo_send.at[i], recv_sem=halo_recv.at[i],
                device_id=neighbour(dy, dx), device_id_type=MESH,
            )
        )

    key = lax.broadcasted_iota(jnp.int32, (512, 128), 0)
    query = lax.broadcasted_iota(jnp.int32, (512, 128), 1)
    off_y = key // 32 - RAD - (7 - query // 16)
    off_x = key % 32 - PAD - query % 16
    inside = (jnp.abs(off_y) <= RAD) & (jnp.abs(off_x) <= RAD)
    maskb[...] = jnp.where(inside, 0.0, LOW)

    for j in range(4):
        acc[j, 0] = jnp.full((8, 512), LOW, F32)
        for s in (1, 2, 3):
            acc[j, s] = jnp.zeros((8, 512), F32)

    def set_bias(j):
        lane = lax.broadcasted_iota(jnp.int32, (NCOLS, 128), 1)
        panel = lax.broadcasted_iota(jnp.int32, (NCOLS, 128), 0)
        column = jnp.sum(jnp.where(lane == panel, lv[j][0:1, :], 0.0), axis=1, keepdims=True)
        biasb[j] = jnp.broadcast_to((1.0 - column) * (2.0 * LOW), (NCOLS, 256))

    def split(j):
        q = qb[j].reshape(BH * BW, CH).astype(F32) * SCALE
        high = q.astype(BF16)
        q2[j] = jnp.concatenate([high, (q - high.astype(F32)).astype(BF16)], axis=1)

    def match(at, panel, tiles):
        keys = kb[at].reshape(BH * BW, CH)
        keys = jnp.concatenate([keys, keys], axis=1)
        base = (panel * BW).astype(F32)
        for j in tiles:
            for lanes in (pl.ds(0, 256), pl.ds(256, 256)):
                score = lax.dot_general(keys, q2[j, lanes, :], NT, preferred_element_type=F32)
                score = score.reshape(64, 8, 256)
                top = jnp.max(score, axis=0)
                level = [jnp.exp2(score[i] - top) for i in range(64)]
                odd = []
                while len(level) > 1:
                    odd.append(functools.reduce(jnp.add, level[1::2]))
                    level = [a + b for a, b in zip(level[0::2], level[1::2])]
                total = level[0]
                in_col = 8.0 * (odd[0] + 2.0 * odd[1] + 4.0 * odd[2]) + base * total
                in_row = odd[3] + 2.0 * odd[4] + 4.0 * odd[5]
                seen = top + biasb[j, pl.ds(panel, 1), :]
                before = acc[j, 0, :, lanes]
                now = jnp.maximum(before, seen)
                keep = jnp.exp2(before - now)
                take = jnp.exp2(seen - now)
                acc[j, 0, :, lanes] = now
                acc[j, 1, :, lanes] = keep * acc[j, 1, :, lanes] + take * total
                acc[j, 2, :, lanes] = keep * acc[j, 2, :, lanes] + take * in_col
                acc[j, 3, :, lanes] = keep * acc[j, 3, :, lanes] + take * in_row

    def window(b, buffer):
        by, bx = b // 8, b % 8
        rows = pl.ds(by * 8, 16)
        keys = ext[rows, pl.ds(pl.multiple_of(bx * 16, 16), 32), :].reshape(512, CH)
        queries = f1v[pl.ds(by * 8, 8), pl.ds(pl.multiple_of(bx * 16, 16), 16), :]
        queries = jnp.concatenate([queries[7 - i] for i in range(8)], axis=0)
        score = lax.dot_general(keys, queries, NT, preferred_element_type=F32) + maskb[...]
        top = jnp.max(score, axis=0, keepdims=True)
        weight = jnp.exp2((score - top) * SCALE)
        total = jnp.sum(weight, axis=0, keepdims=True)
        pairs = weight.reshape(8, 2, 32, 128)
        pairs = (pairs[:, 0] + pairs[:, 1]) * (1.0 / total)
        pscr[buffer] = pairs.reshape(256, 128)
        wbuf[b] = pscr[buffer, pl.ds(0, 128, stride=2), :] + pscr[buffer, pl.ds(1, 128, stride=2), :]

    def some_windows(i, _):
        for n in range(GROUP):
            window(GROUP * i + n, n)
        return 0

    def panel_of(p):
        depth = (p + 1) // 2
        sign = jnp.where(p == 7, -1, 1 - 2 * (p % 2))
        return ylo * 16 + ((z + NZ + sign * depth) % NZ) * 2 + core

    def forward(n):
        d = n // 2
        for i in range(NH // 2):
            h = (n % 2) * (NH // 2) + i
            for way in range(2):
                ring(way, d, h, kb.at[0, 0]).wait_recv()

                @pl.when((d < 2) | (n % 2 == way))
                def _(way=way, h=h):
                    ring(way, d + 1, h, kb.at[1 + 2 * d + way, h]).start()

    set_bias(0)
    own_q.wait()
    split(0)
    own_k.wait()
    match(0, panel_of(0), (0,))
    for h in range(NH // 2, NH):
        for way in range(2):
            ring(way, 0, h, c2.at[h]).start()
    forward(0)
    asks[1].wait_recv()
    asks[2].start()
    forward(1)
    each(halos, "start")
    for j in (1, 2, 3):
        lives[j - 1].wait_recv()
        set_bias(j)
        if j != 2:
            asks[j - 1].wait_recv()
        split(j)
        match(0, panel_of(0), (j,))

    def step(p, _):
        @pl.when(p < 5)
        def _():
            forward(p + 1)

        match(p, panel_of(p), (0, 1, 2, 3))
        return 0

    lax.fori_loop(1, 7, step, 0)
    for i in range(NH // 2):
        for way in range(2):
            ring(way, 3, way * (NH // 2) + i, kb.at[0, 0]).wait_recv()

    sub = lax.broadcasted_iota(jnp.int32, (8, 512), 0).astype(F32)

    def moments(j):
        top8, total, in_col, in_row = acc[j, 0], acc[j, 1], acc[j, 2], acc[j, 3]
        in_col = in_col + sub * total
        top = jnp.max(top8, axis=0, keepdims=True)
        part = jnp.exp2(top8 - top)
        sums = [jnp.sum(part * v, axis=0, keepdims=True) for v in (total, in_col, in_row)]
        return jnp.concatenate([top] + sums + [jnp.zeros((4, 512), F32)], axis=0)

    backs = [share(j, st_tx.at[j - 1], st_rx.at[j - 1], st_send, st_recv) for j in (1, 2, 3)]
    for j in (3, 2, 1):
        match(7, panel_of(7), (j,))
        st_tx[j - 1] = moments(j)
        backs[j - 1].start()
    match(7, panel_of(7), (0,))
    parts = [moments(0)]
    own_f1.wait()
    own_f2.wait()
    each(halos, "wait_recv")
    lax.fori_loop(0, 8 // GROUP, some_windows, 0)
    for j in (1, 2, 3):
        backs[j - 1].wait_recv()
        parts.append(st_rx[j - 1])
    top = functools.reduce(jnp.maximum, [p[0:1] for p in parts])
    scales = [jnp.exp2(p[0:1] - top) for p in parts]
    total, in_col, in_row = (
        functools.reduce(jnp.add, [s * p[i : i + 1] for s, p in zip(scales, parts)]) for i in (1, 2, 3)
    )
    cell = lax.broadcasted_iota(jnp.int32, (1, 512), 1)
    query_col = (c * BW + cell % BW).astype(F32)
    query_row = (cell // BW).astype(F32)
    flow_x = (in_col / total - query_col) * (1.0 / 256.0)
    flow_y = (in_row / total - query_row) * (1.0 / 256.0)
    flow = jnp.concatenate([f[:, 128 * i : 128 * i + 128] for f in (flow_x, flow_y) for i in range(4)], axis=0)
    fl[1, 1] = flow
    edges = []
    for i, (dy, dx) in enumerate(NEIGHBOURS):
        edges.append(
            pltpu.make_async_remote_copy(
                src_ref=fl.at[1, 1], dst_ref=fl.at[1 - dy, 1 - dx],
                send_sem=fl_send.at[i], recv_sem=fl_recv.at[i],
                device_id=neighbour(dy, dx), device_id_type=MESH,
            )
        )
    each(edges, "start")

    for k in range(2):
        for i in range(4):
            pair = flow[k * 4 + i : k * 4 + i + 1, :]
            coarse_out[k, 2 * i : 2 * i + 1, :] = pair[:, :BW]
            coarse_out[k, 2 * i + 1 : 2 * i + 2, :] = pair[:, BW:]
    lax.fori_loop(8 // GROUP, 16 // GROUP, some_windows, 0)

    def spread(k, e, lo, hi, sources):
        shape = (hi - lo, 128)
        row = (e - 2) % 8
        i72 = lax.broadcasted_iota(jnp.int32, shape, 0) + lo
        lane = lax.broadcasted_iota(jnp.int32, shape, 1)
        goal = jnp.where(i72 < 4, 60 + i72, jnp.where(i72 < 68, i72 - 4, i72 - 68)) + (row % 2) * 64
        at = k * 4 + row // 2
        left, mid, right = (s[at : at + 1, :] for s in sources)
        pick = jnp.where(i72 < 4, left, jnp.where(i72 < 68, mid, right))
        value = jnp.sum(jnp.where(lane == goal, pick, 0.0), axis=1, keepdims=True)
        ft[k, e, lo:hi, :] = jnp.broadcast_to(value, shape)

    def weighed(k, b, rows, lo, hi):
        by, bx = b // 8, b % 8
        weight = wbuf[b].reshape(8, 16, 128)[rows.start : rows.stop, lo:hi]
        value = ft[k, by * 4 + rows.start : by * 4 + rows.stop, bx * 8 + lo : bx * 8 + hi, :]
        terms = (weight * value).reshape(-1, 8, 128)
        return functools.reduce(jnp.add, [terms[i] for i in range(terms.shape[0])])

    def inner(b):
        by, bx = b // 8, b % 8
        return (range(2, 8) if by == 0 else range(0, 6)), (8 if bx == 0 else 0), (8 if bx == 7 else 16)

    for k in range(2):
        for e in range(2, 10):
            spread(k, e, 8, 64, (flow, flow, flow))
        for b in range(16):
            part_sum[k, b] = weighed(k, b, *inner(b))

    each(edges, "wait_recv")
    for k in range(2):
        for e in range(12):
            sources = [fl[0 if e < 2 else (1 if e < 10 else 2), tx] for tx in range(3)]
            if 2 <= e < 10:
                spread(k, e, 0, 8, sources)
                spread(k, e, 64, 72, sources)
            else:
                spread(k, e, 0, 72, sources)
    lane8 = lax.broadcasted_iota(jnp.int32, (8, 128), 1)
    sub8 = lax.broadcasted_iota(jnp.int32, (8, 128), 0)
    for k in range(2):
        for by in range(2):
            band = jnp.zeros((8, 128), F32)
            for bx in range(8):
                b = by * 8 + bx
                rows, lo, hi = inner(b)
                value = part_sum[k, b] + weighed(k, b, range(0, 2) if by == 0 else range(6, 8), 0, 16)
                if lo:
                    value = value + weighed(k, b, rows, 0, lo)
                if hi < 16:
                    value = value + weighed(k, b, rows, hi, 16)
                value = jnp.broadcast_to(jnp.sum(value, axis=0, keepdims=True), (8, 128))
                value = pltpu.roll(value, (bx * 16 + 16) % 128, 1)
                band = jnp.where((lane8 // 16 + sub8) % 8 == bx, value, band)
            fine_out[k, by * 8 : by * 8 + 8, :] = pltpu.roll(band, 0, 1, stride=16, stride_axis=0)

    for h in range(NH):
        for way in range(2):
            for d in range(4):
                if d < 3 or h // (NH // 2) == way:
                    ring(way, d, h, kb.at[0, 0]).wait_send()
    for copy in asks + lives + backs:
        copy.wait_send()
    each(halos, "wait_send")
    each(edges, "wait_send")


def local(coarse_one, coarse_two, fine_one, fine_two, selection, counts):
    vm = pltpu.VMEM
    dma = pltpu.SemaphoreType.DMA
    any_spec = pl.BlockSpec(memory_space=pl.ANY)
    vm_spec = pl.BlockSpec(memory_space=pltpu.VMEM)
    coarse, fine = pl.pallas_call(
        kernel,
        out_shape=(jax.ShapeDtypeStruct((2, BH, BW), F32), jax.ShapeDtypeStruct((2, FH, FW), F32)),
        in_specs=[any_spec] * 5 + [pl.BlockSpec(memory_space=pltpu.HBM)],
        out_specs=(vm_spec, vm_spec),
        scratch_shapes=[
            vm((8, NH, BH // NH, BW, CH), BF16),
            vm((4, 2, 4, BW, CH), BF16),
            vm((4, BH * BW, 2 * CH), BF16),
            vm((FH, FW, CH), BF16),
            vm((FH + 2 * RAD, FW + 2 * PAD, CH), BF16),
            vm((16, 128, 128), F32),
            vm((512, 128), F32),
            vm((GROUP, 256, 128), F32),
            vm((12, 1, NCOLS), jnp.int32),
            vm((1, 1), jnp.int32),
            vm((4, 8, 128), F32),
            vm((4, NCOLS, 256), F32),
            vm((4, 4, 8, 512), F32),
            vm((3, 8, 512), F32),
            vm((3, 8, 512), F32),
            vm((3, 3, 8, 128), F32),
            vm((2, 12, 72, 128), F32),
            vm((2, 16, 8, 128), F32),
            dma((2, 4, NH)), dma((2, 4, NH)),
            dma((3,)), dma((3,)), dma((3,)), dma((3,)),
            dma((8,)), dma((8,)),
            dma((3,)), dma((3,)),
            dma((8,)), dma((8,)),
            dma((6,)),
        ],
        compiler_params=pltpu.CompilerParams(collective_id=0, has_side_effects=True, vmem_limit_bytes=55136 << 10),
        name="flow",
    )(
        coarse_one.reshape(2, 4, BW, CH), coarse_two.reshape(NH, BH // NH, BW, CH), fine_one, fine_two,
        selection.reshape(12, 1, NCOLS), counts
    )
    return coarse, fine


def solution(mesh):
    return jax.shard_map(
        local,
        mesh=mesh,
        in_specs=(
            P("rows", "cols", None),
            P("rows", "cols", None),
            P("rows", "cols", None),
            P("rows", "cols", None),
            P("rows", "cols", None, None),
            P("rows", "cols"),
        ),
        out_specs=(P(None, "rows", "cols"), P(None, "rows", "cols")),
        check_vma=False,
    )
```

```python
import functools

import jax
import jax.numpy as jnp
import numpy as np
from jax import lax
from jax.experimental import pallas as pl
from jax.experimental.pallas import tpu as pltpu
from jax.sharding import PartitionSpec as P

MESH = pl.DeviceIdType.MESH
F32 = jnp.float32
BF16 = jnp.bfloat16
NROWS, NCOLS = 8, 32
NZ = 8
GROUP = 4
NH = 4
CH = 128
BH, BW = 8, 64
FH, FW = 16, 128
RAD = 4
PAD = 8
SCALE = float(np.log2(np.e) / np.sqrt(128.0))
LOW = -1.0e30
NEIGHBOURS = [(dy, dx) for dy in (-1, 1, 0) for dx in (-1, 0, 1) if (dy, dx) != (0, 0)]
NT = (((1,), (1,)), ((), ()))


def spans(d, size, halo):
    if d == 0:
        return 0, size, halo
    if d == 1:
        return size - halo, halo, 0
    return 0, halo, size + halo


def kernel(
    c1, c2, f1, f2, sel, cnt,
    coarse_out, fine_out,
    kb, qb, q2, f1v, ext, wbuf, maskb, pscr, selv, cntv, lv, biasb, acc, st_tx, st_rx, fl, ft, part_sum,
    ring_send, ring_recv, q_send, q_recv, lv_send, lv_recv, halo_send, halo_recv,
    st_send, st_recv, fl_send, fl_recv, loc,
):
    r = lax.axis_index("rows")
    c = lax.axis_index("cols")
    ylo = c // 16
    z = (c // 2) % NZ
    core = c % 2

    def at_z(zz):
        return (r, ylo * 16 + zz * 2 + core)

    ring_to = (at_z((z + 1) % NZ), at_z((z + NZ - 1) % NZ))

    def partner(j):
        return (r, ((ylo + j // 2) % 2) * 16 + z * 2 + (core + j % 2) % 2)

    def neighbour(dy, dx):
        return ((r + dy + NROWS) % NROWS, (c + dx + NCOLS) % NCOLS)

    def exists(dy, dx):
        there = True
        for d, at, last in ((dy, r, NROWS - 1), (dx, c, NCOLS - 1)):
            if d == -1:
                there = there & (at > 0)
            if d == 1:
                there = there & (at < last)
        return there

    def each(copies, what):
        for copy, (dy, dx) in zip(copies, NEIGHBOURS):
            there = exists(-dy, -dx) if what == "wait_recv" else exists(dy, dx)

            @pl.when(there)
            def _(copy=copy):
                getattr(copy, what)()

    everyone = list(ring_to) + [partner(j) for j in (1, 2, 3)] + [neighbour(*n) for n in NEIGHBOURS]

    fl[...] = jnp.zeros((3, 3, 8, 128), F32)

    @pl.when(r == 0)
    def _():
        ext[0:RAD] = jnp.zeros((RAD, FW + 2 * PAD, CH), BF16)

    @pl.when(r == NROWS - 1)
    def _():
        ext[RAD + FH :] = jnp.zeros((RAD, FW + 2 * PAD, CH), BF16)

    @pl.when(c == 0)
    def _():
        ext[:, 0:PAD] = jnp.zeros((FH + 2 * RAD, PAD, CH), BF16)

    @pl.when(c == NCOLS - 1)
    def _():
        ext[:, PAD + FW :] = jnp.zeros((FH + 2 * RAD, PAD, CH), BF16)

    barrier = pltpu.get_barrier_semaphore()
    for device in everyone:
        pl.semaphore_signal(barrier, inc=1, device_id=device, device_id_type=MESH)
    own_sel = pltpu.make_async_copy(sel, selv, loc.at[4])
    own_cnt = pltpu.make_async_copy(cnt, cntv, loc.at[5])
    own_k = pltpu.make_async_copy(c2, kb.at[0], loc.at[0])
    own_q = pltpu.make_async_copy(c1, qb.at[0], loc.at[1])
    own_f1 = pltpu.make_async_copy(f1, f1v, loc.at[2])
    own_f2 = pltpu.make_async_copy(f2, ext.at[RAD : RAD + FH, PAD : PAD + FW], loc.at[3])
    for copy in (own_sel, own_cnt, own_k, own_q, own_f1, own_f2):
        copy.start()

    pl.semaphore_wait(barrier, len(everyone))

    def ring(way, d, h, source):
        return pltpu.make_async_remote_copy(
            src_ref=source, dst_ref=kb.at[jnp.minimum(1 + 2 * d + way, 7), h],
            send_sem=ring_send.at[way, d, h], recv_sem=ring_recv.at[way, d, h],
            device_id=ring_to[way], device_id_type=MESH,
        )

    for h in range(NH // 2):
        for way in range(2):
            ring(way, 0, h, c2.at[h]).start()

    def share(j, source, target, send, recv):
        return pltpu.make_async_remote_copy(
            src_ref=source, dst_ref=target, send_sem=send.at[j - 1], recv_sem=recv.at[j - 1],
            device_id=partner(j), device_id_type=MESH,
        )

    lives = [share(j, lv.at[0], lv.at[j], lv_send, lv_recv) for j in (1, 2, 3)]
    asks = [share(1, c1, qb.at[1], q_send, q_recv), share(2, c1, qb.at[2], q_send, q_recv)]
    asks.append(
        pltpu.make_async_remote_copy(
            src_ref=qb.at[2], dst_ref=qb.at[3], send_sem=q_send.at[2], recv_sem=q_recv.at[2],
            device_id=partner(1), device_id_type=MESH,
        )
    )
    asks[1].start()
    asks[0].start()

    own_sel.wait()
    own_cnt.wait()
    slot = lax.broadcasted_iota(jnp.int32, (12, 1, NCOLS), 0)
    chosen = jnp.where(slot < cntv[...].reshape(1, 1, 1), selv[...], 0)
    live = jnp.sum(chosen.astype(F32), axis=0)
    lv[0] = jnp.broadcast_to(jnp.concatenate([live, jnp.zeros((1, 128 - NCOLS), F32)], axis=1), (8, 128))

    for copy in lives:
        copy.start()

    halos = []
    for i, (dy, dx) in enumerate(NEIGHBOURS):
        ys, yn, yt = spans(dy, FH, RAD)
        xs, xn, xt = spans(dx, FW, PAD)
        halos.append(
            pltpu.make_async_remote_copy(
                src_ref=f2.at[ys : ys + yn, xs : xs + xn], dst_ref=ext.at[yt : yt + yn, xt : xt + xn],
                send_sem=halo_send.at[i], recv_sem=halo_recv.at[i],
                device_id=neighbour(dy, dx), device_id_type=MESH,
            )
        )

    key = lax.broadcasted_iota(jnp.int32, (512, 128), 0)
    query = lax.broadcasted_iota(jnp.int32, (512, 128), 1)
    off_y = key // 32 - RAD - (7 - query // 16)
    off_x = key % 32 - PAD - query % 16
    inside = (jnp.abs(off_y) <= RAD) & (jnp.abs(off_x) <= RAD)
    maskb[...] = jnp.where(inside, 0.0, LOW)

    for j in range(4):
        acc[j, 0] = jnp.full((8, 512), LOW, F32)
        for s in (1, 2, 3):
            acc[j, s] = jnp.zeros((8, 512), F32)

    def set_bias(j):
        lane = lax.broadcasted_iota(jnp.int32, (NCOLS, 128), 1)
        panel = lax.broadcasted_iota(jnp.int32, (NCOLS, 128), 0)
        column = jnp.sum(jnp.where(lane == panel, lv[j][0:1, :], 0.0), axis=1, keepdims=True)
        biasb[j] = jnp.broadcast_to((1.0 - column) * (2.0 * LOW), (NCOLS, 256))

    def split(j):
        q = qb[j].reshape(BH * BW, CH).astype(F32) * SCALE
        high = q.astype(BF16)
        q2[j] = jnp.concatenate([high, (q - high.astype(F32)).astype(BF16)], axis=1)

    def match(at, panel, tiles):
        keys = kb[at].reshape(BH * BW, CH)
        keys = jnp.concatenate([keys, keys], axis=1)
        base = (panel * BW).astype(F32)
        for j in tiles:
            for lanes in (pl.ds(0, 256), pl.ds(256, 256)):
                score = lax.dot_general(keys, q2[j, lanes, :], NT, preferred_element_type=F32)
                score = score.reshape(64, 8, 256)
                top = jnp.max(score, axis=0)
                level = [jnp.exp2(score[i] - top) for i in range(64)]
                odd = []
                while len(level) > 1:
                    odd.append(functools.reduce(jnp.add, level[1::2]))
                    level = [a + b for a, b in zip(level[0::2], level[1::2])]
                total = level[0]
                in_col = 8.0 * (odd[0] + 2.0 * odd[1] + 4.0 * odd[2]) + base * total
                in_row = odd[3] + 2.0 * odd[4] + 4.0 * odd[5]
                seen = top + biasb[j, pl.ds(panel, 1), :]
                before = acc[j, 0, :, lanes]
                now = jnp.maximum(before, seen)
                keep = jnp.exp2(before - now)
                take = jnp.exp2(seen - now)
                acc[j, 0, :, lanes] = now
                acc[j, 1, :, lanes] = keep * acc[j, 1, :, lanes] + take * total
                acc[j, 2, :, lanes] = keep * acc[j, 2, :, lanes] + take * in_col
                acc[j, 3, :, lanes] = keep * acc[j, 3, :, lanes] + take * in_row

    def window(b, buffer):
        by, bx = b // 8, b % 8
        rows = pl.ds(by * 8, 16)
        keys = ext[rows, pl.ds(pl.multiple_of(bx * 16, 16), 32), :].reshape(512, CH)
        queries = f1v[pl.ds(by * 8, 8), pl.ds(pl.multiple_of(bx * 16, 16), 16), :]
        queries = jnp.concatenate([queries[7 - i] for i in range(8)], axis=0)
        score = lax.dot_general(keys, queries, NT, preferred_element_type=F32) + maskb[...]
        top = jnp.max(score, axis=0, keepdims=True)
        weight = jnp.exp2((score - top) * SCALE)
        total = jnp.sum(weight, axis=0, keepdims=True)
        pairs = weight.reshape(8, 2, 32, 128)
        pairs = (pairs[:, 0] + pairs[:, 1]) * (1.0 / total)
        pscr[buffer] = pairs.reshape(256, 128)
        wbuf[b] = pscr[buffer, pl.ds(0, 128, stride=2), :] + pscr[buffer, pl.ds(1, 128, stride=2), :]

    def some_windows(i, _):
        for n in range(GROUP):
            window(GROUP * i + n, n)
        return 0

    def panel_of(p):
        depth = (p + 1) // 2
        sign = jnp.where(p == 7, -1, 1 - 2 * (p % 2))
        return ylo * 16 + ((z + NZ + sign * depth) % NZ) * 2 + core

    def forward(n):
        d = n // 2
        for i in range(NH // 2):
            h = (n % 2) * (NH // 2) + i
            for way in range(2):
                ring(way, d, h, kb.at[0, 0]).wait_recv()

                @pl.when((d < 2) | (n % 2 == way))
                def _(way=way, h=h):
                    ring(way, d + 1, h, kb.at[1 + 2 * d + way, h]).start()

    set_bias(0)
    own_q.wait()
    split(0)
    own_k.wait()
    match(0, panel_of(0), (0,))
    for h in range(NH // 2, NH):
        for way in range(2):
            ring(way, 0, h, c2.at[h]).start()
    forward(0)
    asks[1].wait_recv()
    asks[2].start()
    forward(1)
    each(halos, "start")
    for j in (1, 2, 3):
        lives[j - 1].wait_recv()
        set_bias(j)
        if j != 2:
            asks[j - 1].wait_recv()
        split(j)
        match(0, panel_of(0), (j,))

    def step(p, _):
        @pl.when(p < 5)
        def _():
            forward(p + 1)

        match(p, panel_of(p), (0, 1, 2, 3))
        return 0

    lax.fori_loop(1, 7, step, 0)
    for i in range(NH // 2):
        for way in range(2):
            ring(way, 3, way * (NH // 2) + i, kb.at[0, 0]).wait_recv()

    sub = lax.broadcasted_iota(jnp.int32, (8, 512), 0).astype(F32)

    def moments(j):
        top8, total, in_col, in_row = acc[j, 0], acc[j, 1], acc[j, 2], acc[j, 3]
        in_col = in_col + sub * total
        top = jnp.max(top8, axis=0, keepdims=True)
        part = jnp.exp2(top8 - top)
        sums = [jnp.sum(part * v, axis=0, keepdims=True) for v in (total, in_col, in_row)]
        return jnp.concatenate([top] + sums + [jnp.zeros((4, 512), F32)], axis=0)

    backs = [share(j, st_tx.at[j - 1], st_rx.at[j - 1], st_send, st_recv) for j in (1, 2, 3)]
    for j in (3, 2, 1):
        match(7, panel_of(7), (j,))
        st_tx[j - 1] = moments(j)
        backs[j - 1].start()
    match(7, panel_of(7), (0,))
    parts = [moments(0)]
    own_f1.wait()
    own_f2.wait()
    each(halos, "wait_recv")
    lax.fori_loop(0, 4 // GROUP, some_windows, 0)
    for j in (1, 2, 3):
        backs[j - 1].wait_recv()
        parts.append(st_rx[j - 1])
    top = functools.reduce(jnp.maximum, [p[0:1] for p in parts])
    scales = [jnp.exp2(p[0:1] - top) for p in parts]
    total, in_col, in_row = (
        functools.reduce(jnp.add, [s * p[i : i + 1] for s, p in zip(scales, parts)]) for i in (1, 2, 3)
    )
    cell = lax.broadcasted_iota(jnp.int32, (1, 512), 1)
    query_col = (c * BW + cell % BW).astype(F32)
    query_row = (cell // BW).astype(F32)
    flow_x = (in_col / total - query_col) * (1.0 / 256.0)
    flow_y = (in_row / total - query_row) * (1.0 / 256.0)
    flow = jnp.concatenate([f[:, 128 * i : 128 * i + 128] for f in (flow_x, flow_y) for i in range(4)], axis=0)
    fl[1, 1] = flow
    edges = []
    for i, (dy, dx) in enumerate(NEIGHBOURS):
        edges.append(
            pltpu.make_async_remote_copy(
                src_ref=fl.at[1, 1], dst_ref=fl.at[1 - dy, 1 - dx],
                send_sem=fl_send.at[i], recv_sem=fl_recv.at[i],
                device_id=neighbour(dy, dx), device_id_type=MESH,
            )
        )
    each(edges, "start")

    for k in range(2):
        for i in range(4):
            pair = flow[k * 4 + i : k * 4 + i + 1, :]
            coarse_out[k, 2 * i : 2 * i + 1, :] = pair[:, :BW]
            coarse_out[k, 2 * i + 1 : 2 * i + 2, :] = pair[:, BW:]
    lax.fori_loop(4 // GROUP, 16 // GROUP, some_windows, 0)

    def spread(k, e, lo, hi, sources):
        shape = (hi - lo, 128)
        row = (e - 2) % 8
        i72 = lax.broadcasted_iota(jnp.int32, shape, 0) + lo
        lane = lax.broadcasted_iota(jnp.int32, shape, 1)
        goal = jnp.where(i72 < 4, 60 + i72, jnp.where(i72 < 68, i72 - 4, i72 - 68)) + (row % 2) * 64
        at = k * 4 + row // 2
        left, mid, right = (s[at : at + 1, :] for s in sources)
        pick = jnp.where(i72 < 4, left, jnp.where(i72 < 68, mid, right))
        value = jnp.sum(jnp.where(lane == goal, pick, 0.0), axis=1, keepdims=True)
        ft[k, e, lo:hi, :] = jnp.broadcast_to(value, shape)

    def weighed(k, b, rows, lo, hi):
        by, bx = b // 8, b % 8
        weight = wbuf[b].reshape(8, 16, 128)[rows.start : rows.stop, lo:hi]
        value = ft[k, by * 4 + rows.start : by * 4 + rows.stop, bx * 8 + lo : bx * 8 + hi, :]
        terms = (weight * value).reshape(-1, 8, 128)
        return functools.reduce(jnp.add, [terms[i] for i in range(terms.shape[0])])

    def inner(b):
        by, bx = b // 8, b % 8
        return (range(2, 8) if by == 0 else range(0, 6)), (8 if bx == 0 else 0), (8 if bx == 7 else 16)

    for k in range(2):
        for e in range(2, 10):
            spread(k, e, 8, 64, (flow, flow, flow))
        for b in range(16):
            part_sum[k, b] = weighed(k, b, *inner(b))

    each(edges, "wait_recv")
    for k in range(2):
        for e in range(12):
            sources = [fl[0 if e < 2 else (1 if e < 10 else 2), tx] for tx in range(3)]
            if 2 <= e < 10:
                spread(k, e, 0, 8, sources)
                spread(k, e, 64, 72, sources)
            else:
                spread(k, e, 0, 72, sources)
    lane8 = lax.broadcasted_iota(jnp.int32, (8, 128), 1)
    sub8 = lax.broadcasted_iota(jnp.int32, (8, 128), 0)
    for k in range(2):
        for by in range(2):
            band = jnp.zeros((8, 128), F32)
            for bx in range(8):
                b = by * 8 + bx
                rows, lo, hi = inner(b)
                value = part_sum[k, b] + weighed(k, b, range(0, 2) if by == 0 else range(6, 8), 0, 16)
                if lo:
                    value = value + weighed(k, b, rows, 0, lo)
                if hi < 16:
                    value = value + weighed(k, b, rows, hi, 16)
                value = jnp.broadcast_to(jnp.sum(value, axis=0, keepdims=True), (8, 128))
                value = pltpu.roll(value, (bx * 16 + 16) % 128, 1)
                band = jnp.where((lane8 // 16 + sub8) % 8 == bx, value, band)
            fine_out[k, by * 8 : by * 8 + 8, :] = pltpu.roll(band, 0, 1, stride=16, stride_axis=0)

    for h in range(NH):
        for way in range(2):
            for d in range(4):
                if d < 3 or h // (NH // 2) == way:
                    ring(way, d, h, kb.at[0, 0]).wait_send()
    for copy in asks + lives + backs:
        copy.wait_send()
    each(halos, "wait_send")
    each(edges, "wait_send")


def local(coarse_one, coarse_two, fine_one, fine_two, selection, counts):
    vm = pltpu.VMEM
    dma = pltpu.SemaphoreType.DMA
    any_spec = pl.BlockSpec(memory_space=pl.ANY)
    vm_spec = pl.BlockSpec(memory_space=pltpu.VMEM)
    coarse, fine = pl.pallas_call(
        kernel,
        out_shape=(jax.ShapeDtypeStruct((2, BH, BW), F32), jax.ShapeDtypeStruct((2, FH, FW), F32)),
        in_specs=[any_spec] * 5 + [pl.BlockSpec(memory_space=pltpu.HBM)],
        out_specs=(vm_spec, vm_spec),
        scratch_shapes=[
            vm((8, NH, BH // NH, BW, CH), BF16),
            vm((4, 2, 4, BW, CH), BF16),
            vm((4, BH * BW, 2 * CH), BF16),
            vm((FH, FW, CH), BF16),
            vm((FH + 2 * RAD, FW + 2 * PAD, CH), BF16),
            vm((16, 128, 128), F32),
            vm((512, 128), F32),
            vm((GROUP, 256, 128), F32),
            vm((12, 1, NCOLS), jnp.int32),
            vm((1, 1), jnp.int32),
            vm((4, 8, 128), F32),
            vm((4, NCOLS, 256), F32),
            vm((4, 4, 8, 512), F32),
            vm((3, 8, 512), F32),
            vm((3, 8, 512), F32),
            vm((3, 3, 8, 128), F32),
            vm((2, 12, 72, 128), F32),
            vm((2, 16, 8, 128), F32),
            dma((2, 4, NH)), dma((2, 4, NH)),
            dma((3,)), dma((3,)), dma((3,)), dma((3,)),
            dma((8,)), dma((8,)),
            dma((3,)), dma((3,)),
            dma((8,)), dma((8,)),
            dma((6,)),
        ],
        compiler_params=pltpu.CompilerParams(collective_id=0, has_side_effects=True, vmem_limit_bytes=55136 << 10),
        name="flow",
    )(
        coarse_one.reshape(2, 4, BW, CH), coarse_two.reshape(NH, BH // NH, BW, CH), fine_one, fine_two,
        selection.reshape(12, 1, NCOLS), counts
    )
    return coarse, fine


def solution(mesh):
    return jax.shard_map(
        local,
        mesh=mesh,
        in_specs=(
            P("rows", "cols", None),
            P("rows", "cols", None),
            P("rows", "cols", None),
            P("rows", "cols", None),
            P("rows", "cols", None, None),
            P("rows", "cols"),
        ),
        out_specs=(P(None, "rows", "cols"), P(None, "rows", "cols")),
        check_vma=False,
    )
```
